32 devices in a mesh: rollout: 4 (over y, core), row: 2 (over x), col: 4 (over z).
Axes of the slice: x: 2, y: 2, z: 4, core: 2. Of those that a mesh axis runs over, the one named last changes fastest.
Arguments:
- queries: bfloat16 [4096, 4096], P(('rollout', 'row', 'col')), may hold values from -16 to 16
- keys: bfloat16 [4096, 512], P(('rollout', 'row', 'col')), may hold values from -16 to 16
- values: bfloat16 [4096, 512], P(('rollout', 'row', 'col')), may hold values from -6 to 6
- out_grad: bfloat16 [4096, 4096], P(('rollout', 'row', 'col')), may hold values from -12 to 12
- hidden_in: bfloat16 [4096, 8192], P(('rollout', 'col'), 'row'), may hold values from -1.5 to 1.5
- q_weight: bfloat16 [4096, 8192], P('col', 'row'), may hold values from -0.09375 to 0.09375
- lengths: int32 [4, 32], P('rollout'), may hold values from 1 to 64, 1024 in all within a row
- kv_order: int32 [4], replicated, may hold values from 0 to 3, each once
Outputs:
- key_grad: float32 [4096, 512], P(('rollout', 'row', 'col'))
- value_grad: float32 [4096, 512], P(('rollout', 'row', 'col'))
- input_grad: bfloat16 [4096, 8192], P(('rollout', 'col'), 'row')
- weight_grad: float32 [4096, 8192], P(('rollout', 'col'), 'row')
The draws below stay inside these ranges and needn't reach their ends.
Inputs may be any that keep to these rules, and one draw needn't show every extreme that they name: `lengths`: each row lists, for 16 packed rollouts in order, a prompt length and then a response length; a row sums to 1024 and its largest entry is exactly 64. `kv_order`: A permutation of the 4 key-value heads.
All inputs are finite; a program needn't handle non-finite values.
Results may differ from the reference program's by a relative error of at most 0.0057.
Values may be sent and summed in bfloat16 or wider, within the bound.
A program may use at most 192 MiB of HBM per device.

```python
import math
import jax
import jax.numpy as jnp
import numpy as np
from jax import lax

D = 8192
HQ = 32
KV = 4
HD = 128
ROLLS = 16
GROUPS = 4
TOK_G = 1024
TOKENS = 4096
MOST = 64
N_ROLLOUT = 4


def paired_draw(key):
    query_key = jax.random.fold_in(key, 101)
    key_key = jax.random.fold_in(key, 202)
    query_vals = jnp.clip(jax.random.normal(query_key, (TOKENS, HQ * HD), jnp.float32), -4.0, 4.0)
    key_vals = jnp.clip(jax.random.normal(key_key, (TOKENS, KV * HD), jnp.float32), -4.0, 4.0)
    return (query_vals, key_vals)


def draw_queries(key, part):
    return paired_draw(key)[0].astype(jnp.bfloat16)


def draw_keys(key, part):
    return paired_draw(key)[1].astype(jnp.bfloat16)


def block_scale(key, extent, shards, smallest, high):
    gain, own = 1.0, jax.random.fold_in(key, 6)
    for dim, blocks in shards:
        draws = jnp.exp(jax.random.uniform(jax.random.fold_in(own, dim), (blocks,), jnp.float32, smallest / len(shards), high / len(shards)))
        gain = gain * jnp.repeat(draws, extent[dim] // blocks).reshape([-1 if axis == dim else 1 for axis in range(len(extent))])
    return gain


def profile(amount, total, most, skew):
    loads = [(1 << 20) // math.isqrt(rank ** skew) + 1 for rank in range(2, amount + 1)]
    spare, holding = total - most - (amount - 1), [1] * (amount - 1)
    while spare > 0:
        free = [i for i in range(amount - 1) if holding[i] < most]
        pool, remaining = sum([loads[i] for i in free]), spare
        for i in free:
            extra = min(most - holding[i], max(1, remaining * loads[i] // pool), spare)
            holding[i] = holding[i] + extra
            spare = spare - extra
    return np.array([most] + holding)


def uneven(key, count, total, bound, skew):
    if count == 2:
        one = jax.random.randint(key, (), max(1, total - bound), min(bound, total - 1) + 1)
        return jnp.stack([one, total - one])
    sizes = jnp.asarray(profile(count, total, bound, skew), jnp.int32)
    couples = (count - 1) // 2
    giver, receiver = sizes[1:1 + 2 * couples:2], sizes[2:2 + 2 * couples:2]
    slack = jnp.minimum(giver - 1, bound - receiver)
    shifted = jax.random.randint(jax.random.fold_in(key, 1), (couples,), 0, 1 << 20) % (slack + 1)
    sizes = sizes.at[1:1 + 2 * couples:2].set(giver - shifted).at[2:2 + 2 * couples:2].set(receiver + shifted)
    return sizes[jax.random.permutation(jax.random.fold_in(key, 2), count)]


def gaussian(key, shape, scale, most, cuts=(), held_as=jnp.bfloat16):
    gain = block_scale(key, shape, cuts, -0.22, 0.18) if cuts else 1.0
    values = jax.random.normal(key, shape, jnp.float32) * scale * gain
    return jnp.minimum(jnp.maximum(values, -most), most).astype(held_as)


def setup_inputs(seed: int = 0) -> dict:
    splits = jax.random.split(jax.random.key(seed), 9)
    return {
        "queries": draw_queries(jax.random.fold_in(splits[8], 71), 0),
        "keys": draw_keys(jax.random.fold_in(splits[8], 71), 0),
        "values": gaussian(splits[2], (TOKENS, KV * HD), 1.0, 6.0, ((0, 32),)),
        "out_grad": gaussian(splits[3], (TOKENS, HQ * HD), 2.0, 12.0, ((0, 32),)),
        "hidden_in": gaussian(splits[4], (TOKENS, D), 0.25, 1.5, ((0, 16), (1, 2))),
        "q_weight": gaussian(splits[5], (HQ * HD, D), (HQ * HD) ** -0.5, 0.09375, ((0, 4), (1, 2))),
        "lengths": jax.vmap(lambda own: uneven(own, 2 * ROLLS, TOK_G, MOST, 1))(jax.random.split(splits[6], GROUPS)).reshape((GROUPS, 2 * ROLLS)).astype(jnp.int32),
        "kv_order": jax.random.permutation(splits[7], KV).astype(jnp.int32),
    }


def token_parts(lengths_row, length_total):
    bounds = jnp.cumsum(lengths_row).astype(jnp.int32)
    position = jnp.arange(length_total, dtype=jnp.int32)
    return lax.optimization_barrier(jnp.sum((position[:, None] >= bounds[None, :]).astype(jnp.int32), axis=1)).astype(jnp.int32)

def group_grads(queries, keys, values, out_grad, lengths_row, kv_order):
    scale_factor = 1.0 / math.sqrt(HD)
    parts = token_parts(lengths_row, TOK_G)
    document = parts // 2
    response = (parts % 2).astype(jnp.bfloat16)
    position = jnp.arange(TOK_G, dtype=jnp.int32)
    allowed = (position[None, :] <= position[:, None]) & (document[None, :] == document[:, None])
    masked = out_grad * response[:, None]
    kv_of_head = kv_order[jnp.arange(HQ, dtype=jnp.int32) // (HQ // KV)].astype(jnp.int32)
    query_heads = queries.reshape(TOK_G, HQ, HD).transpose(1, 0, 2)
    grad_heads = masked.reshape(TOK_G, HQ, HD).transpose(1, 0, 2)
    key_heads = jnp.take(keys.reshape(TOK_G, KV, HD).transpose(1, 0, 2), kv_of_head, axis=0)
    value_heads = jnp.take(values.reshape(TOK_G, KV, HD).transpose(1, 0, 2), kv_of_head, axis=0)

    def one_head(operands):
        query_rows, key_rows, value_rows, grad_rows = operands
        raw_scores = jnp.dot(query_rows, key_rows.T, preferred_element_type=jnp.float32) * scale_factor
        raw_scores = jnp.where(allowed, raw_scores, -jnp.inf)
        row_top = lax.optimization_barrier(jnp.max(raw_scores, axis=1, keepdims=True))
        exp_scores = jnp.exp(raw_scores - row_top)
        attention = exp_scores / lax.optimization_barrier(jnp.sum(exp_scores, axis=1, keepdims=True))
        attention_half = attention.astype(jnp.bfloat16)
        grad_value = jnp.dot(attention_half.T, grad_rows, preferred_element_type=jnp.float32)
        grad_attention = jnp.dot(grad_rows, value_rows.T, preferred_element_type=jnp.float32)
        row_delta = lax.optimization_barrier(jnp.sum(attention * grad_attention, axis=1, keepdims=True))
        grad_scores = (attention * (grad_attention - row_delta) * scale_factor).astype(jnp.bfloat16)
        grad_query = jnp.dot(grad_scores, key_rows, preferred_element_type=jnp.float32).astype(jnp.bfloat16)
        grad_key = jnp.dot(grad_scores.T, query_rows, preferred_element_type=jnp.float32)
        return (grad_query, grad_key, grad_value)
    head_query, head_key, head_value = lax.map(one_head, (query_heads, key_heads, value_heads, grad_heads))
    query_grad = head_query.transpose(1, 0, 2).reshape(TOK_G, HQ * HD)
    key_list = []
    value_list = []
    for kv_index in range(KV):
        chosen = (kv_of_head == kv_index)[:, None, None]
        key_list.append(lax.optimization_barrier(jnp.sum(jnp.where(chosen, head_key, jnp.zeros_like(head_key)), axis=0)))
        value_list.append(lax.optimization_barrier(jnp.sum(jnp.where(chosen, head_value, jnp.zeros_like(head_value)), axis=0)))
    key_grad = jnp.stack(key_list, axis=1).reshape(TOK_G, KV * HD)
    value_grad = jnp.stack(value_list, axis=1).reshape(TOK_G, KV * HD)
    return (query_grad, key_grad, value_grad)

def reference(queries, keys, values, out_grad, hidden_in, q_weight, lengths, kv_order):
    key_parts = []
    value_parts = []
    input_parts = []
    weight_grad = jnp.zeros((HQ * HD, D), jnp.float32)
    for rollout_group in range(N_ROLLOUT):
        row_first = rollout_group * TOK_G
        row_last = row_first + TOK_G
        query_grad, key_grad, value_grad = group_grads(queries[row_first:row_last], keys[row_first:row_last], values[row_first:row_last], out_grad[row_first:row_last], lengths[rollout_group], kv_order)
        key_parts.append(key_grad)
        value_parts.append(value_grad)
        input_parts.append(jnp.dot(query_grad, q_weight, preferred_element_type=jnp.float32).astype(jnp.bfloat16))
        weight_grad = weight_grad + jnp.dot(query_grad.T, hidden_in[row_first:row_last], preferred_element_type=jnp.float32)
    return (jnp.concatenate(key_parts, axis=0), jnp.concatenate(value_parts, axis=0), jnp.concatenate(input_parts, axis=0), weight_grad)
```

```python
import functools
import math

import jax
import jax.numpy as jnp
from jax import lax
from jax.experimental import pallas as pl
from jax.experimental.pallas import tpu as pltpu
from jax.sharding import PartitionSpec as P

HQ = 32
KV = 4
HD = 128
ROLLS = 16
NJ = 4
MESH = pl.DeviceIdType.MESH


def dot32(a, b):
    return jnp.dot(a, b, preferred_element_type=jnp.float32)


def dot_nt(a, b):
    return lax.dot_general(a, b, (((1,), (1,)), ((), ())), preferred_element_type=jnp.float32)


def dot_tn(a, b):
    return lax.dot_general(a, b, (((0,), (0,)), ((), ())), preferred_element_type=jnp.float32)


def step_kernel(
    sizes,
    order_ref, lengths_ref, q_hbm, k_hbm, v_hbm, g_hbm, h_hbm, w_hbm,
    kg_ref, vg_ref, ig_hbm, wg_hbm,
    qv, gv, kb, vb, bias, resp, dq2, a1, a2, a2t, hid, wv, rs, w1s, w1r, w2s, w2r, wo, dka, dks, dkr,
    s_in, s_halo, r_halo, s_g, r_g, s_q1, r_q1, s_f1, s_q2, r_q2, s_f2, s_rs, r_rs, s_w1, r_w1, s_w2, r_w2, s_dk, r_dk, s_ig, s_wo,
):
    nc, nr, td, tb, fp, fb, dj, nh = sizes
    z, row, ro = lax.axis_index("col"), lax.axis_index("row"), lax.axis_index("rollout")
    dev = row * nc + z
    group = nr * nc
    kw = KV * HD
    scale = 1.0 / math.sqrt(HD)
    core, yside = ro ^ 1, ro ^ 2

    def at(d):
        return {"row": d // nc, "col": d % nc}

    own = pl.ds(nh * td, td)
    loads = [
        pltpu.make_async_copy(k_hbm, kb.at[own, :], s_in.at[0]),
        pltpu.make_async_copy(v_hbm, vb.at[own, :], s_in.at[1]),
        pltpu.make_async_copy(q_hbm, qv, s_in.at[2]),
        pltpu.make_async_copy(g_hbm, gv, s_in.at[3]),
    ]
    for j in range(NJ):
        loads.append(
            pltpu.make_async_copy(
                h_hbm.at[:, pl.ds(j * dj, dj)], hid.at[j, pl.ds(pl.multiple_of(z * tb, tb), tb), :], s_in.at[4 + j]
            )
        )
        loads.append(pltpu.make_async_copy(w_hbm.at[:, pl.ds(j * dj, dj)], wv.at[j], s_in.at[4 + NJ + j]))
    for copy in loads:
        copy.start()

    barrier = pltpu.get_barrier_semaphore()
    for c in range(1, nc):
        pl.semaphore_signal(barrier, inc=1, device_id={"col": (z + c) % nc}, device_id_type=MESH)
    for r in range(1, nr):
        pl.semaphore_signal(barrier, inc=1, device_id={"row": (row + r) % nr}, device_id_type=MESH)
    pl.semaphore_signal(barrier, inc=1, device_id={"rollout": core}, device_id_type=MESH)
    pl.semaphore_signal(barrier, inc=1, device_id={"rollout": yside}, device_id_type=MESH)
    for h in range(1, nh + 1):
        @pl.when(dev >= h)
        def _(h=h):
            pl.semaphore_signal(barrier, inc=1, device_id=at(dev - h), device_id_type=MESH)

        @pl.when(dev + h < group)
        def _(h=h):
            pl.semaphore_signal(barrier, inc=1, device_id=at(dev + h), device_id_type=MESH)
    peers = nc - 1 + nr - 1 + 2
    for h in range(1, nh + 1):
        peers = peers + jnp.where(dev >= h, 1, 0) + jnp.where(dev + h < group, 1, 0)
    pl.semaphore_wait(barrier, peers)

    def halo(h, i):
        src, dst = ((k_hbm, kb), (v_hbm, vb))[i]
        return pltpu.make_async_remote_copy(
            src_ref=src, dst_ref=dst.at[pl.ds((nh - h) * td, td), :],
            send_sem=s_halo.at[h - 1, i], recv_sem=r_halo.at[h - 1, i],
            device_id=at(lax.rem(dev + h, group)), device_id_type=MESH,
        )

    for h in range(1, nh + 1):
        @pl.when(dev + h < group)
        def _(h=h):
            halo(h, 0).start()
            halo(h, 1).start()

    def plane_rows(p):
        return pl.ds(pl.multiple_of(p * tb, tb), tb)

    def gather(up, hop, j):
        plane = z - (hop - 1) if up else z + (hop - 1)
        src = h_hbm.at[:, pl.ds(pl.multiple_of(j * dj, dj), dj)] if hop == 1 else hid.at[j, plane_rows(plane), :]
        return pltpu.make_async_remote_copy(
            src_ref=src, dst_ref=hid.at[j, plane_rows(plane), :],
            send_sem=s_g.at[0 if up else 1, hop - 1, j], recv_sem=r_g.at[0 if up else 1, hop - 1, j],
            device_id={"col": z + 1 if up else z - 1}, device_id_type=MESH,
        )

    def gather_sends(up, hop):
        return (z < nc - 1) & (z >= hop - 1) if up else (z > 0) & (z + hop - 1 < nc)

    def gather_lands(up, hop):
        return z >= hop if up else z + hop < nc

    def gather_start(hop, j):
        for up in (True, False):
            @pl.when(gather_sends(up, hop))
            def _(up=up):
                gather(up, hop, j).start()

    def gather_wait(hop, j):
        for up in (True, False):
            @pl.when(gather_lands(up, hop))
            def _(up=up):
                plane = z - hop if up else z + hop
                pltpu.make_async_remote_copy(
                    src_ref=hid.at[j, plane_rows(plane), :], dst_ref=hid.at[j, plane_rows(plane), :],
                    send_sem=s_g.at[0 if up else 1, hop - 1, j], recv_sem=r_g.at[0 if up else 1, hop - 1, j],
                    device_id={"col": z}, device_id_type=MESH,
                ).wait_recv()

    early = NJ // 2
    for j in range(early):
        gather_start(1, j)

    pos = dev * td + lax.broadcasted_iota(jnp.int32, (td, 1), 0)
    bound, parts, start = jnp.int32(0), jnp.zeros((td, 1), jnp.int32), jnp.zeros((td, 1), jnp.int32)
    for i in range(2 * ROLLS):
        bound = bound + lengths_ref[0, i]
        reached = pos >= bound
        parts = parts + reached.astype(jnp.int32)
        if i % 2:
            start = jnp.where(reached, bound, start)
    resp[...] = (parts % 2).astype(jnp.float32)
    shape = (td, (nh + 1) * td)
    col = lax.broadcasted_iota(jnp.int32, shape, 1) + (dev - nh) * td
    line = lax.broadcasted_iota(jnp.int32, shape, 0) + dev * td
    bias[...] = jnp.where((col <= line) & (col >= start), 0.0, -jnp.inf)

    for h in range(1, nh + 1):
        rows = pl.ds((nh - h) * td, td)

        @pl.when(dev < h)
        def _(rows=rows):
            kb[rows, :] = jnp.zeros((td, kw), kb.dtype)
            vb[rows, :] = jnp.zeros((td, kw), vb.dtype)

        @pl.when(dev >= h)
        def _(h=h):
            halo(h, 0).wait_recv()
            halo(h, 1).wait_recv()
    for copy in loads[:4]:
        copy.wait()

    per = HQ // KV

    def send_q1(p):
        return pltpu.make_async_remote_copy(
            src_ref=qv.at[:, pl.ds(pl.multiple_of(p * fp, fp), fp)],
            dst_ref=a1.at[pl.ds(pl.multiple_of(dev * td, td), td), :],
            send_sem=s_q1.at[p], recv_sem=r_q1.at[dev],
            device_id={"col": p}, device_id_type=MESH,
        )

    def block(m, _):
        reads = jnp.full((1, HD), order_ref[m], jnp.int32)
        k = jnp.zeros(((nh + 1) * td, HD), jnp.float32)
        v = jnp.zeros(((nh + 1) * td, HD), jnp.float32)
        for c in range(KV):
            k = jnp.where(reads == c, kb[:, c * HD : (c + 1) * HD].astype(jnp.float32), k)
            v = jnp.where(reads == c, vb[:, c * HD : (c + 1) * HD].astype(jnp.float32), v)
        k, v = k.astype(jnp.bfloat16), v.astype(jnp.bfloat16)
        dk = jnp.zeros(((nh + 1) * td, HD), jnp.float32)
        dv = jnp.zeros(((nh + 1) * td, HD), jnp.float32)
        for hh in range(per):
            cols = pl.ds(pl.multiple_of((m * per + hh) * HD, HD), HD)
            q = qv[:, cols]
            g = (gv[:, cols].astype(jnp.float32) * resp[...]).astype(jnp.bfloat16)
            s = dot_nt(q, k) * scale + bias[...]
            e = jnp.exp(s - jnp.max(s, axis=1, keepdims=True))
            p = e * (1.0 / jnp.sum(e, axis=1, keepdims=True))
            dp = dot_nt(g, v)
            delta = jnp.sum(p * dp, axis=1, keepdims=True)
            ds = (p * (dp - delta) * scale).astype(jnp.bfloat16)
            qv[:, cols] = dot32(ds, k).astype(jnp.bfloat16)
            dk = dk + dot_tn(ds, q)
            dv = dv + dot_tn(p.astype(jnp.bfloat16), g)
        dka[:, pl.ds(pl.multiple_of(m * HD, HD), HD)] = dk
        dka[:, pl.ds(pl.multiple_of(kw + m * HD, HD), HD)] = dv
        if nc == KV:
            @pl.when(m != z)
            def _():
                send_q1(m).start()
        return 0

    lax.fori_loop(0, KV, block, 0)
    if nc != KV:
        for c in range(1, nc):
            send_q1((z + c) % nc).start()

    for p in range(nc):
        for b in range(1, nc):
            o = (p + b) % nc
            dq2[p, :, (b - 1) * fb : b * fb] = qv[:, o * fp + p * fb : o * fp + (p + 1) * fb]

    def send_q2(p):
        return pltpu.make_async_remote_copy(
            src_ref=dq2.at[p], dst_ref=a2.at[pl.ds(pl.multiple_of(dev * td, td), td), pl.ds(fb, (nc - 1) * fb)],
            send_sem=s_q2.at[p], recv_sem=r_q2.at[dev],
            device_id={"col": p}, device_id_type=MESH,
        )

    for c in range(1, nc):
        send_q2((z + c) % nc).start()

    def dk_copy(h):
        return pltpu.make_async_remote_copy(
            src_ref=dks.at[h - 1], dst_ref=dkr.at[h - 1], send_sem=s_dk.at[h - 1], recv_sem=r_dk.at[h - 1],
            device_id=at(lax.rem(dev - h + group, group)), device_id_type=MESH,
        )

    for h in range(1, nh + 1):
        dks[h - 1] = dka[(nh - h) * td : (nh - h + 1) * td, :].astype(jnp.bfloat16)

        @pl.when(dev >= h)
        def _(h=h):
            dk_copy(h).start()

    for j in range(early, NJ):
        gather_start(1, j)

    def piece(d):
        return pl.ds(pl.multiple_of(d * td, td), td)

    def over1(d, r):
        return pltpu.make_async_remote_copy(
            src_ref=a1.at[piece(d), :], dst_ref=a1.at[piece(d), :], send_sem=s_f1.at[d % nc, r], recv_sem=r_q1.at[d],
            device_id={"row": (row + r) % nr}, device_id_type=MESH,
        )

    def over2(d, r):
        return pltpu.make_async_remote_copy(
            src_ref=a2.at[piece(d), pl.ds(fb, (nc - 1) * fb)], dst_ref=a2.at[piece(d), pl.ds(fb, (nc - 1) * fb)],
            send_sem=s_f2.at[d % nc, r], recv_sem=r_q2.at[d],
            device_id={"row": (row + r) % nr}, device_id_type=MESH,
        )

    a1[piece(dev), :] = qv[:, pl.ds(pl.multiple_of(z * fp, fp), fp)]
    a2[piece(dev), pl.ds(fb, (nc - 1) * fb)] = dq2[z]
    for over in (over1, over2):
        for r in range(1, nr):
            over(dev, r).start()
        for c in (1, -1, 2, -2, 3, -3) if nc == 4 else range(1, nc):
            other = z + c if nc == 4 else (z + c) % nc

            @pl.when((other >= 0) & (other < nc))
            def _(over=over, other=other):
                d = row * nc + other
                over(d, 0).wait_recv()
                for r in range(1, nr):
                    over(d, r).start()
    for over in (over1, over2):
        for r in range(1, nr):
            for c in range(nc):
                over(((row + r) % nr) * nc + c, 0).wait_recv()
    a2[:, 0:fb] = a1[:, pl.ds(pl.multiple_of(z * fb, fb), fb)]
    for r in range(group * td // tb):
        rows = slice(r * tb, (r + 1) * tb)
        a2t[:, rows] = a2[rows, :].T

    def slot(up, t):
        return jnp.where(up == 0, t - 1, t)

    def rs_copy(way, t, j):
        at_slot = rs.at[way, slot(way, t), j]
        return pltpu.make_async_remote_copy(
            src_ref=at_slot, dst_ref=at_slot, send_sem=s_rs.at[way, slot(way, t), j], recv_sem=r_rs.at[way, slot(way, t), j],
            device_id={"col": jnp.where(way == 0, z + 1, z - 1)}, device_id_type=MESH,
        )

    def term(t, j):
        return dot32(a1[plane_rows(t), :], wv[j])

    def rs_sends(j):
        def one(i, _):
            way = i % 2
            t = jnp.where(way == 0, nc - 1 - i // 2, i // 2)
            lands = jnp.where(way == 0, z > 0, z < nc - 1)
            sends = jnp.where(way == 0, t > z, t < z)

            @pl.when(sends)
            def _():
                part = term(t, j)

                @pl.when(lands)
                def _():
                    rs_copy(way, t, j).wait_recv()
                    rs[way, slot(way, t), j] = (part + rs[way, slot(way, t), j].astype(jnp.float32)).astype(jnp.bfloat16)

                @pl.when(jnp.logical_not(lands))
                def _():
                    rs[way, slot(way, t), j] = part.astype(jnp.bfloat16)

                rs_copy(way, t, j).start()
            return 0

        lax.fori_loop(0, 2 * (nc - 1), one, 0)

    way_z, slot_z = jnp.where(z > 0, 0, 1), jnp.where(z > 0, z - 1, 0)

    def ig_copy(j):
        return pltpu.make_async_copy(
            rs.at[way_z, slot_z, j], ig_hbm.at[:, pl.ds(pl.multiple_of(j * dj, dj), dj)], s_ig.at[j]
        )

    def rs_final(j):
        part = term(z, j)

        @pl.when(z > 0)
        def _():
            rs_copy(0, z, j).wait_recv()

        @pl.when(z < nc - 1)
        def _():
            rs_copy(1, z, j).wait_recv()

        first = part + rs[way_z, slot_z, j].astype(jnp.float32)

        @pl.when((z > 0) & (z < nc - 1))
        def _():
            rs[0, z - 1, j] = (first + rs[1, z, j].astype(jnp.float32)).astype(jnp.bfloat16)

        @pl.when((z == 0) | (z == nc - 1))
        def _():
            rs[way_z, slot_z, j] = first.astype(jnp.bfloat16)

        ig_copy(j).start()

    def wterm(o, j):
        b = lax.rem(o - z + nc, nc)
        return dot32(a2t[pl.ds(pl.multiple_of(b * fb, fb), fb), :], hid[j])

    def w1_copy(i, j):
        return pltpu.make_async_remote_copy(
            src_ref=w1s.at[i, j], dst_ref=w1r.at[i, j], send_sem=s_w1.at[i, j], recv_sem=r_w1.at[i, j],
            device_id={"rollout": core}, device_id_type=MESH,
        )

    def w2_copy(j):
        return pltpu.make_async_remote_copy(
            src_ref=w2s.at[j], dst_ref=w2r.at[j], send_sem=s_w2.at[j], recv_sem=r_w2.at[j],
            device_id={"rollout": yside}, device_id_type=MESH,
        )

    def wo_copy(j):
        return pltpu.make_async_copy(wo.at[j], wg_hbm.at[:, pl.ds(pl.multiple_of(j * dj, dj), dj)], s_wo.at[j])

    def weight1(j):
        gather_wait(nc - 1, j)

        def one(i, _):
            w1s[i, j] = wterm(core ^ (2 * i), j).astype(jnp.bfloat16)
            w1_copy(i, j).start()
            return 0

        lax.fori_loop(0, 2, one, 0)

    def weight2(j):
        part = wterm(yside, j)
        w1_copy(1, j).wait_recv()
        w2s[j] = (part + w1r[1, j].astype(jnp.float32)).astype(jnp.bfloat16)
        w2_copy(j).start()

    def weight3(j):
        part = wterm(ro, j)
        w1_copy(0, j).wait_recv()
        w2_copy(j).wait_recv()
        wo[j] = part + w1r[0, j].astype(jnp.float32) + w2r[j].astype(jnp.float32)
        wo_copy(j).start()

    def relay(hop, j):
        gather_wait(hop, j)
        gather_start(hop + 1, j)

    for copy in loads[4:]:
        copy.wait()
    relay(1, 0)

    def step(j, _):
        for hop in range(2, nc - 1):
            @pl.when(j < NJ)
            def _(hop=hop):
                relay(hop, j)

        @pl.when(j < NJ - 1)
        def _():
            relay(1, j + 1)

        @pl.when(j < NJ)
        def _():
            rs_sends(j)

        @pl.when((j >= 1) & (j <= NJ))
        def _():
            rs_final(j - 1)
            weight1(j - 1)

        @pl.when((j >= 2) & (j <= NJ + 1))
        def _():
            weight2(j - 2)

        @pl.when(j >= 3)
        def _():
            weight3(j - 3)
        return 0

    lax.fori_loop(0, NJ + 3, step, 0)

    for h in range(1, nh + 1):
        @pl.when(dev + h < group)
        def _(h=h):
            dk_copy(h).wait_recv()
            dka[pl.ds(nh * td, td), :] = dka[pl.ds(nh * td, td), :] + dkr[h - 1].astype(jnp.float32)
    for out, first in ((kg_ref, 0), (vg_ref, kw)):
        for c in range(KV):
            total = jnp.zeros((td, HD), jnp.float32)
            for m in range(KV):
                mine = dka[pl.ds(nh * td, td), first + m * HD : first + (m + 1) * HD]
                total = jnp.where(jnp.full((1, HD), order_ref[m], jnp.int32) == c, mine, total)
            out[:, c * HD : (c + 1) * HD] = total

    for h in range(1, nh + 1):
        @pl.when(dev + h < group)
        def _(h=h):
            halo(h, 0).wait_send()
            halo(h, 1).wait_send()

        @pl.when(dev >= h)
        def _(h=h):
            dk_copy(h).wait_send()
    for c in range(1, nc):
        send_q1((z + c) % nc).wait_send()
        send_q2((z + c) % nc).wait_send()
    for over in (over1, over2):
        for r in range(1, nr):
            for c in range(nc):
                over(row * nc + c, r).wait_send()

    def drain(j, _):
        for hop in range(1, nc):
            for up in (True, False):
                @pl.when(gather_sends(up, hop))
                def _(hop=hop, up=up):
                    gather(up, hop, j).wait_send()
        for way in range(2):
            for t in range(way == 0, nc - way):
                @pl.when(t > z if way == 0 else t < z)
                def _(way=way, t=t):
                    rs_copy(way, t, j).wait_send()
        for i in range(2):
            w1_copy(i, j).wait_send()
        w2_copy(j).wait_send()
        ig_copy(j).wait()
        wo_copy(j).wait()
        return 0

    lax.fori_loop(0, NJ, drain, 0)


def body(queries, keys, values, out_grad, hidden_in, q_weight, lengths, kv_order):
    nr, nc, nro = lax.axis_size("row"), lax.axis_size("col"), lax.axis_size("rollout")
    td, group = queries.shape[0], nr * nc
    length = td * group
    tb, width = hidden_in.shape
    fp = q_weight.shape[0]
    fb = fp // nro
    dj = width // NJ
    nh = -(-(2 * (length // ROLLS) - 1) // td)
    kw = KV * HD
    bf, f32, dma = jnp.bfloat16, jnp.float32, pltpu.SemaphoreType.DMA
    hbm, smem, vmem = (pl.BlockSpec(memory_space=m) for m in (pl.ANY, pltpu.SMEM, pltpu.VMEM))
    call = pl.pallas_call(
        functools.partial(step_kernel, (nc, nr, td, tb, fp, fb, dj, nh)),
        out_shape=(
            jax.ShapeDtypeStruct((td, kw), f32),
            jax.ShapeDtypeStruct((td, kw), f32),
            jax.ShapeDtypeStruct((tb, width), bf),
            jax.ShapeDtypeStruct((fb, width), f32),
        ),
        in_specs=[smem, smem] + [hbm] * 6,
        out_specs=(vmem, vmem, hbm, hbm),
        scratch_shapes=[
            pltpu.VMEM((td, HQ * HD), bf),
            pltpu.VMEM((td, HQ * HD), bf),
            pltpu.VMEM(((nh + 1) * td, kw), bf),
            pltpu.VMEM(((nh + 1) * td, kw), bf),
            pltpu.VMEM((td, (nh + 1) * td), f32),
            pltpu.VMEM((td, 1), f32),
            pltpu.VMEM((nc, td, (nc - 1) * fb), bf),
            pltpu.VMEM((length, fp), bf),
            pltpu.VMEM((length, nc * fb), bf),
            pltpu.VMEM((nc * fb, length), bf),
            pltpu.VMEM((NJ, length, dj), bf),
            pltpu.VMEM((NJ, fp, dj), bf),
            pltpu.VMEM((2, nc - 1, NJ, tb, dj), bf),
            pltpu.VMEM((2, NJ, fb, dj), bf),
            pltpu.VMEM((2, NJ, fb, dj), bf),
            pltpu.VMEM((NJ, fb, dj), bf),
            pltpu.VMEM((NJ, fb, dj), bf),
            pltpu.VMEM((NJ, fb, dj), f32),
            pltpu.VMEM(((nh + 1) * td, 2 * kw), f32),
            pltpu.VMEM((nh, td, 2 * kw), bf),
            pltpu.VMEM((nh, td, 2 * kw), bf),
            dma((4 + 2 * NJ,)),
            dma((nh, 2)), dma((nh, 2)),
            dma((2, nc - 1, NJ)), dma((2, nc - 1, NJ)),
            dma((nc,)), dma((group,)), dma((nc, nr)),
            dma((nc,)), dma((group,)), dma((nc, nr)),
            dma((2, nc - 1, NJ)), dma((2, nc - 1, NJ)),
            dma((2, NJ)), dma((2, NJ)), dma((NJ,)), dma((NJ,)),
            dma((nh,)), dma((nh,)), dma((NJ,)), dma((NJ,)),
        ],
        compiler_params=pltpu.CompilerParams(
            collective_id=0, has_side_effects=True, vmem_limit_bytes=67043328
        ),
        name="step",
    )
    return call(kv_order, lengths, queries, keys, values, out_grad, hidden_in, q_weight)


def solution(mesh):
    return jax.shard_map(
        body,
        mesh=mesh,
        in_specs=(
            P(("rollout", "row", "col"), None),
            P(("rollout", "row", "col"), None),
            P(("rollout", "row", "col"), None),
            P(("rollout", "row", "col"), None),
            P(("rollout", "col"), "row"),
            P("col", "row"),
            P("rollout", None),
            P(),
        ),
        out_specs=(
            P(("rollout", "row", "col"), None),
            P(("rollout", "row", "col"), None),
            P(("rollout", "col"), "row"),
            P(("rollout", "col"), "row"),
        ),
        check_vma=False,
    )
```

```python
import functools
import math

import jax
import jax.numpy as jnp
from jax import lax
from jax.experimental import pallas as pl
from jax.experimental.pallas import tpu as pltpu
from jax.sharding import PartitionSpec as P

HQ = 32
KV = 4
HD = 128
ROLLS = 16
CHUNKS = 8
PIECES = 8
EARLY = 4
MORE = 6
FIRST = 2
LEAD1 = 2
LEAD2 = 1
MESH = pl.DeviceIdType.MESH


def dot32(a, b):
    return jnp.dot(a, b, preferred_element_type=jnp.float32)


def dot_nt(a, b):
    return lax.dot_general(a, b, (((1,), (1,)), ((), ())), preferred_element_type=jnp.float32)


def dot_tn(a, b):
    return lax.dot_general(a, b, (((0,), (0,)), ((), ())), preferred_element_type=jnp.float32)


def step_kernel(
    sizes,
    order_ref, lengths_ref, q_hbm, k_hbm, v_hbm, g_hbm, h_hbm, w_hbm,
    kv_ref, ig_hbm, wg_hbm,
    qv, gv, kb, vb, bias, resp, dq2, a1, a2, a2t, hid, wv, rs, w1s, w1r, w2s, w2r, wo, dka, dks, dkr,
    s_in, s_halo, r_halo, s_g, r_g, s_q1, r_q1, s_f1, s_q2, r_q2, s_f2, s_rs, r_rs, s_w1, r_w1, s_w2, r_w2, s_dk, r_dk, s_ig, s_wo,
):
    nc, nr, td, tb, fp, fb, dj, nh, nj = sizes
    early, first, lead1, lead2 = (max(1, x * nj // CHUNKS) for x in (EARLY, FIRST, LEAD1, LEAD2))
    z, row, ro = lax.axis_index("col"), lax.axis_index("row"), lax.axis_index("rollout")
    dev = row * nc + z
    group = nr * nc
    kw = KV * HD
    scale = 1.0 / math.sqrt(HD)
    core, yside = ro ^ 1, ro ^ 2

    def at(d):
        return {"row": d // nc, "col": d % nc}

    own = pl.ds(nh * td, td)
    loads = [
        pltpu.make_async_copy(k_hbm, kb.at[own, :], s_in.at[0]),
        pltpu.make_async_copy(v_hbm, vb.at[own, :], s_in.at[1]),
        pltpu.make_async_copy(q_hbm, qv, s_in.at[2]),
        pltpu.make_async_copy(g_hbm, gv, s_in.at[3]),
    ]
    own_rows = pl.ds(pl.multiple_of(z * tb, tb), tb)
    for j in range(nj):
        loads.append(pltpu.make_async_copy(h_hbm.at[:, pl.ds(j * dj, dj)], hid.at[j, own_rows, :], s_in.at[4]))
        loads.append(pltpu.make_async_copy(w_hbm.at[:, pl.ds(j * dj, dj)], wv.at[j], s_in.at[5 + j * 4 // nj]))
    for copy in loads:
        copy.start()

    barrier = pltpu.get_barrier_semaphore()
    for c in range(1, nc):
        pl.semaphore_signal(barrier, inc=1, device_id={"col": (z + c) % nc}, device_id_type=MESH)
    for r in range(1, nr):
        pl.semaphore_signal(barrier, inc=1, device_id={"row": (row + r) % nr}, device_id_type=MESH)
    pl.semaphore_signal(barrier, inc=1, device_id={"rollout": core}, device_id_type=MESH)
    pl.semaphore_signal(barrier, inc=1, device_id={"rollout": yside}, device_id_type=MESH)
    for h in range(1, nh + 1):
        @pl.when(dev >= h)
        def _(h=h):
            pl.semaphore_signal(barrier, inc=1, device_id=at(dev - h), device_id_type=MESH)

        @pl.when(dev + h < group)
        def _(h=h):
            pl.semaphore_signal(barrier, inc=1, device_id=at(dev + h), device_id_type=MESH)
    peers = nc - 1 + nr - 1 + 2
    for h in range(1, nh + 1):
        peers = peers + jnp.where(dev >= h, 1, 0) + jnp.where(dev + h < group, 1, 0)
    pl.semaphore_wait(barrier, peers)

    def halo(h, i):
        src, dst = ((k_hbm, kb), (v_hbm, vb))[i]
        return pltpu.make_async_remote_copy(
            src_ref=src, dst_ref=dst.at[pl.ds((nh - h) * td, td), :],
            send_sem=s_halo.at[h - 1, i], recv_sem=r_halo.at[h - 1, i],
            device_id=at(lax.rem(dev + h, group)), device_id_type=MESH,
        )

    for h in range(1, nh + 1):
        @pl.when(dev + h < group)
        def _(h=h):
            halo(h, 0).start()
            halo(h, 1).start()

    def plane_rows(p):
        return pl.ds(pl.multiple_of(p * tb, tb), tb)

    def gather(up, hop, j):
        plane = z - (hop - 1) if up else z + (hop - 1)
        src = h_hbm.at[:, pl.ds(pl.multiple_of(j * dj, dj), dj)] if hop == 1 else hid.at[j, plane_rows(plane), :]
        return pltpu.make_async_remote_copy(
            src_ref=src, dst_ref=hid.at[j, plane_rows(plane), :],
            send_sem=s_g.at[0 if up else 1, hop - 1], recv_sem=r_g.at[0 if up else 1, hop - 1, j],
            device_id={"col": z + 1 if up else z - 1}, device_id_type=MESH,
        )

    def gather_sends(up, hop):
        return (z < nc - 1) & (z >= hop - 1) if up else (z > 0) & (z + hop - 1 < nc)

    def gather_lands(up, hop):
        return z >= hop if up else z + hop < nc

    def gather_start(hop, j):
        for up in (True, False):
            @pl.when(gather_sends(up, hop))
            def _(up=up):
                gather(up, hop, j).start()

    def gather_wait(hop, j, relays):
        for up in (True, False):
            on = gather_sends(up, hop + 1) if hop < nc - 1 else jnp.bool_(False)
            on = on if relays else jnp.logical_not(on)

            @pl.when(gather_lands(up, hop) & on)
            def _(up=up):
                plane = z - hop if up else z + hop
                pltpu.make_async_remote_copy(
                    src_ref=hid.at[j, plane_rows(plane), :], dst_ref=hid.at[j, plane_rows(plane), :],
                    send_sem=s_g.at[0 if up else 1, hop - 1], recv_sem=r_g.at[0 if up else 1, hop - 1, j],
                    device_id={"col": z}, device_id_type=MESH,
                ).wait_recv()

    for j in range(first):
        gather_start(1, j)

    pos = dev * td + lax.broadcasted_iota(jnp.int32, (td, 1), 0)
    bound, parts, start = jnp.int32(0), jnp.zeros((td, 1), jnp.int32), jnp.zeros((td, 1), jnp.int32)
    for i in range(2 * ROLLS):
        bound = bound + lengths_ref[0, i]
        reached = pos >= bound
        parts = parts + reached.astype(jnp.int32)
        if i % 2:
            start = jnp.where(reached, bound, start)
    resp[...] = (parts % 2).astype(jnp.float32)
    shape = (td, (nh + 1) * td)
    col = lax.broadcasted_iota(jnp.int32, shape, 1) + (dev - nh) * td
    line = lax.broadcasted_iota(jnp.int32, shape, 0) + dev * td
    bias[...] = jnp.where((col <= line) & (col >= start), 0.0, -jnp.inf)

    for h in range(1, nh + 1):
        rows = pl.ds((nh - h) * td, td)

        @pl.when(dev < h)
        def _(rows=rows):
            kb[rows, :] = jnp.zeros((td, kw), kb.dtype)
            vb[rows, :] = jnp.zeros((td, kw), vb.dtype)

        @pl.when(dev >= h)
        def _(h=h):
            halo(h, 0).wait_recv()
            halo(h, 1).wait_recv()
    for copy in loads[:4]:
        copy.wait()

    per = HQ // KV

    def send_q1(p):
        return pltpu.make_async_remote_copy(
            src_ref=qv.at[:, pl.ds(pl.multiple_of(p * fp, fp), fp)],
            dst_ref=a1.at[pl.ds(pl.multiple_of(dev * td, td), td), :],
            send_sem=s_q1.at[p], recv_sem=r_q1.at[dev],
            device_id={"col": p}, device_id_type=MESH,
        )

    def nth(i):
        return jnp.where(z < nc // 2, KV - 1 - i, i)

    def block(i, _):
        m = jnp.where(i == KV - 1, z, jnp.where(nth(i) == z, nth(KV - 1), nth(i))) if nc == KV else i
        reads = jnp.full((1, HD), order_ref[m], jnp.int32)
        k = jnp.zeros(((nh + 1) * td, HD), jnp.float32)
        v = jnp.zeros(((nh + 1) * td, HD), jnp.float32)
        for c in range(KV):
            k = jnp.where(reads == c, kb[:, c * HD : (c + 1) * HD].astype(jnp.float32), k)
            v = jnp.where(reads == c, vb[:, c * HD : (c + 1) * HD].astype(jnp.float32), v)
        k, v = k.astype(jnp.bfloat16), v.astype(jnp.bfloat16)
        dk = jnp.zeros(((nh + 1) * td, HD), jnp.float32)
        dv = jnp.zeros(((nh + 1) * td, HD), jnp.float32)
        for hh in range(per):
            cols = pl.ds(pl.multiple_of((m * per + hh) * HD, HD), HD)
            q = qv[:, cols]
            g = (gv[:, cols].astype(jnp.float32) * resp[...]).astype(jnp.bfloat16)
            s = dot_nt(q, k) * scale + bias[...]
            e = jnp.exp(s - jnp.max(s, axis=1, keepdims=True))
            p = e * (1.0 / jnp.sum(e, axis=1, keepdims=True))
            dp = dot_nt(g, v)
            delta = jnp.sum(p * dp, axis=1, keepdims=True)
            ds = (p * (dp - delta) * scale).astype(jnp.bfloat16)
            qv[:, cols] = dot32(ds, k).astype(jnp.bfloat16)
            dk = dk + dot_tn(ds, q)
            dv = dv + dot_tn(p.astype(jnp.bfloat16), g)
        dka[:, pl.ds(pl.multiple_of(m * HD, HD), HD)] = dk
        dka[:, pl.ds(pl.multiple_of(kw + m * HD, HD), HD)] = dv
        if nc == KV:
            @pl.when(m != z)
            def _():
                send_q1(m).start()
        return 0

    lax.fori_loop(0, KV, block, 0)
    if nc != KV:
        for c in range(1, nc):
            send_q1((z + c) % nc).start()

    for p in range(nc):
        for b in range(1, nc):
            o = (p + b) % nc
            dq2[p, :, (b - 1) * fb : b * fb] = qv[:, o * fp + p * fb : o * fp + (p + 1) * fb]

    def send_q2(p):
        return pltpu.make_async_remote_copy(
            src_ref=dq2.at[p], dst_ref=a2.at[pl.ds(pl.multiple_of(dev * td, td), td), :],
            send_sem=s_q2.at[p], recv_sem=r_q2.at[dev],
            device_id={"col": p}, device_id_type=MESH,
        )

    for j in range(first, early):
        gather_start(1, j)
    inner = (z > 0) & (z < nc - 1)

    def send_second():
        for c in range(1, nc):
            send_q2((z + c) % nc).start()

    def dk_copy(h):
        return pltpu.make_async_remote_copy(
            src_ref=dks.at[h - 1], dst_ref=dkr.at[h - 1], send_sem=s_dk.at[h - 1], recv_sem=r_dk.at[h - 1],
            device_id=at(lax.rem(dev - h + group, group)), device_id_type=MESH,
        )

    for h in range(1, nh + 1):
        dks[h - 1] = dka[(nh - h) * td : (nh - h + 1) * td, :].astype(jnp.bfloat16)

        @pl.when(dev >= h)
        def _(h=h):
            dk_copy(h).start()

    def piece(d):
        return pl.ds(pl.multiple_of(d * td, td), td)

    def over1(d, r):
        return pltpu.make_async_remote_copy(
            src_ref=a1.at[piece(d), :], dst_ref=a1.at[piece(d), :], send_sem=s_f1.at[d % nc, r], recv_sem=r_q1.at[d],
            device_id={"row": (row + r) % nr}, device_id_type=MESH,
        )

    def over2(d, r):
        return pltpu.make_async_remote_copy(
            src_ref=a2.at[piece(d), :], dst_ref=a2.at[piece(d), :],
            send_sem=s_f2.at[d % nc, r], recv_sem=r_q2.at[d],
            device_id={"row": (row + r) % nr}, device_id_type=MESH,
        )

    def spread(over):
        for r in range(1, nr):
            over(dev, r).start()
        for c in (2, -2, 3, -3, 1, -1) if nc == 4 else range(1, nc):
            other = z + c if nc == 4 else (z + c) % nc

            @pl.when((other >= 0) & (other < nc))
            def _(other=other):
                d = row * nc + other
                over(d, 0).wait_recv()
                for r in range(1, nr):
                    over(d, r).start()

    def landed(over):
        for r in range(1, nr):
            for c in range(nc):
                over(((row + r) % nr) * nc + c, 0).wait_recv()

    a1[piece(dev), :] = qv[:, pl.ds(pl.multiple_of(z * fp, fp), fp)]
    a2[piece(dev), :] = dq2[z]
    spread(over1)

    more = max(1, MORE * nj // CHUNKS)

    @pl.when(inner)
    def _():
        send_second()
        for j in range(early, more):
            gather_start(1, j)

    landed(over1)

    def second_map():
        landed(over2)
        for r in range(group * td // tb):
            rows = slice(r * tb, (r + 1) * tb)
            a2t[0:fb, rows] = a1[rows, pl.ds(pl.multiple_of(z * fb, fb), fb)].T
            a2t[fb:, rows] = a2[rows, :].T

    def slot(up, t):
        return jnp.where(up == 0, t - 1, t)

    def rs_copy(way, t, j):
        at_slot = rs.at[way, slot(way, t), j]
        return pltpu.make_async_remote_copy(
            src_ref=at_slot, dst_ref=at_slot, send_sem=s_rs.at[way, slot(way, t)], recv_sem=r_rs.at[way, slot(way, t), j],
            device_id={"col": jnp.where(way == 0, z + 1, z - 1)}, device_id_type=MESH,
        )

    def term(t, j):
        return dot32(a1[plane_rows(t), :], wv[j])

    def rs_sends(j, first, last):
        def one(i, _):
            way = (i + z // (nc // 2)) % 2
            t = jnp.where(way == 0, nc - 1 - i // 2, i // 2)
            lands = jnp.where(way == 0, z > 0, z < nc - 1)
            sends = jnp.where(way == 0, t > z, t < z)

            @pl.when(sends)
            def _():
                part = term(t, j)

                @pl.when(lands)
                def _():
                    rs_copy(way, t, j).wait_recv()
                    rs[way, slot(way, t), j] = (part + rs[way, slot(way, t), j].astype(jnp.float32)).astype(jnp.bfloat16)

                @pl.when(jnp.logical_not(lands))
                def _():
                    rs[way, slot(way, t), j] = part.astype(jnp.bfloat16)

                rs_copy(way, t, j).start()
            return 0

        lax.fori_loop(first, last, one, 0)

    way_z, slot_z = jnp.where(z > 0, 0, 1), jnp.where(z > 0, z - 1, 0)

    def ig_copy(j):
        return pltpu.make_async_copy(
            rs.at[way_z, slot_z, j], ig_hbm.at[:, pl.ds(pl.multiple_of(j * dj, dj), dj)], s_ig.at[0]
        )

    def rs_final(j):
        part = term(z, j)

        @pl.when(z > 0)
        def _():
            rs_copy(0, z, j).wait_recv()

        @pl.when(z < nc - 1)
        def _():
            rs_copy(1, z, j).wait_recv()

        first = part + rs[way_z, slot_z, j].astype(jnp.float32)

        @pl.when((z > 0) & (z < nc - 1))
        def _():
            rs[0, z - 1, j] = (first + rs[1, z, j].astype(jnp.float32)).astype(jnp.bfloat16)

        @pl.when((z == 0) | (z == nc - 1))
        def _():
            rs[way_z, slot_z, j] = first.astype(jnp.bfloat16)

        ig_copy(j).start()

    def wterm(o, j):
        b = lax.rem(o - z + nc, nc)
        return dot32(a2t[pl.ds(pl.multiple_of(b * fb, fb), fb), :], hid[j])

    def w1_copy(i, j):
        return pltpu.make_async_remote_copy(
            src_ref=w1s.at[i, j], dst_ref=w1r.at[i, j], send_sem=s_w1.at[i], recv_sem=r_w1.at[i, j],
            device_id={"rollout": core}, device_id_type=MESH,
        )

    def w2_copy(j):
        return pltpu.make_async_remote_copy(
            src_ref=w2s.at[j], dst_ref=w2r.at[j], send_sem=s_w2.at[0], recv_sem=r_w2.at[j],
            device_id={"rollout": yside}, device_id_type=MESH,
        )

    def wo_copy(j):
        return pltpu.make_async_copy(wo.at[j], wg_hbm.at[:, pl.ds(pl.multiple_of(j * dj, dj), dj)], s_wo.at[j * 2 // nj])

    def weight1(j):
        for hop in range(1, nc):
            gather_wait(hop, j, False)

        def one(i, _):
            w1s[i, j] = wterm(core ^ (2 * i), j).astype(jnp.bfloat16)
            w1_copy(i, j).start()
            return 0

        lax.fori_loop(0, 2, one, 0)

    def weight2(j):
        part = wterm(yside, j)
        w1_copy(1, j).wait_recv()
        w2s[j] = (part + w1r[1, j].astype(jnp.float32)).astype(jnp.bfloat16)
        w2_copy(j).start()

    def weight3(j):
        part = wterm(ro, j)
        w1_copy(0, j).wait_recv()
        w2_copy(j).wait_recv()
        wo[j] = part + w1r[0, j].astype(jnp.float32) + w2r[j].astype(jnp.float32)
        wo_copy(j).start()

    def relay(hop, j):
        gather_wait(hop, j, True)
        gather_start(hop + 1, j)

    pltpu.make_async_copy(hid.at[:, own_rows, :], hid.at[:, own_rows, :], s_in.at[4]).wait()
    for i in range(4):
        quarter = wv.at[pl.ds(i * nj // 4, nj // 4)]
        pltpu.make_async_copy(quarter, quarter, s_in.at[5 + i]).wait()
    for j in range(lead1):
        relay(1, j)

    def step(j, _):
        @pl.when(j < nj - lead1)
        def _():
            relay(1, j + lead1)

        begun = j + jnp.where(inner, more, early)

        @pl.when(begun < nj)
        def _():
            gather_start(1, begun)

        @pl.when(j < nj)
        def _():
            rs_sends(j, 0, 2)

        for hop in range(2, nc - 1):
            @pl.when(j == 0)
            def _(hop=hop):
                for i in range(lead2):
                    relay(hop, i)

            @pl.when(j < nj - lead2)
            def _(hop=hop):
                relay(hop, j + lead2)

        @pl.when(j < nj)
        def _():
            rs_sends(j, 2, 2 * (nc - 1))

        @pl.when(j == 0)
        def _():
            @pl.when(jnp.logical_not(inner))
            def _():
                send_second()

            spread(over2)

        @pl.when(j == 1)
        def _():
            second_map()

        @pl.when(inner & (j == 1))
        def _():
            weight1(0)
            weight1(1)
            weight2(0)

        ahead = j + jnp.where(inner, 1, -1)

        @pl.when((j >= 1) & (ahead < nj))
        def _():
            weight1(ahead)

        @pl.when((ahead >= jnp.where(inner, 2, 1)) & (ahead <= nj))
        def _():
            weight2(ahead - 1)

        @pl.when(j >= 3)
        def _():
            rs_final(j - 3)

        behind = j - jnp.where(inner, 2, 3)

        @pl.when((behind >= 0) & (behind < nj))
        def _():
            weight3(behind)
        return 0

    lax.fori_loop(0, nj + 3, step, 0)

    for h in range(1, nh + 1):
        @pl.when(dev + h < group)
        def _(h=h):
            dk_copy(h).wait_recv()
            dka[pl.ds(nh * td, td), :] = dka[pl.ds(nh * td, td), :] + dkr[h - 1].astype(jnp.float32)
    kv_ref[...] = dka[pl.ds(nh * td, td), :]

    for h in range(1, nh + 1):
        @pl.when(dev + h < group)
        def _(h=h):
            halo(h, 0).wait_send()
            halo(h, 1).wait_send()

        @pl.when(dev >= h)
        def _(h=h):
            dk_copy(h).wait_send()
    for c in range(1, nc):
        send_q1((z + c) % nc).wait_send()
        send_q2((z + c) % nc).wait_send()
    for over in (over1, over2):
        for r in range(1, nr):
            for c in range(nc):
                over(row * nc + c, r).wait_send()

    def sent(ref, sem):
        pltpu.make_async_copy(ref, ref, sem).wait()

    for hop in range(1, nc):
        for up in (True, False):
            @pl.when(gather_sends(up, hop))
            def _(hop=hop, up=up):
                sent(hid.at[:, own_rows, :], s_g.at[0 if up else 1, hop - 1])
    for way in range(2):
        for t in range(way == 0, nc - way):
            @pl.when(t > z if way == 0 else t < z)
            def _(way=way, t=t):
                sent(rs.at[0, 0], s_rs.at[way, slot(way, t)])
    for i in range(2):
        sent(w1s.at[i], s_w1.at[i])
    sent(w2s, s_w2.at[0])
    sent(rs.at[0, 0], s_ig.at[0])
    for i in range(2):
        sent(wo.at[pl.ds(i * nj // 2, nj // 2)], s_wo.at[i])


def place_kernel(order_ref, kv_hbm, ig_hbm, wg_hbm, kg_out, vg_out, ig_out, wg_out, kv, placed, ig, wg, s_in, s_out):
    kw = kv.shape[1] // 2
    whole = pltpu.make_async_copy(kv_hbm, kv, s_in.at[0, 0])
    whole.start()
    moves = []
    for p in range(PIECES):
        for i, (src, mid, out) in enumerate(((ig_hbm, ig, ig_out), (wg_hbm, wg, wg_out))):
            rows = pl.ds(p * (mid.shape[0] // PIECES), mid.shape[0] // PIECES)
            into = pltpu.make_async_copy(src.at[rows, :], mid.at[rows, :], s_in.at[1 + i, p])
            into.start()
            moves.append((into, pltpu.make_async_copy(mid.at[rows, :], out.at[rows, :], s_out.at[i, p])))
    whole.wait()
    for c in range(KV):
        for first in (0, kw):
            total = jnp.zeros((kv.shape[0], HD), jnp.float32)
            for m in range(KV):
                mine = kv[:, first + m * HD : first + (m + 1) * HD]
                total = jnp.where(jnp.full((1, HD), order_ref[m], jnp.int32) == c, mine, total)
            placed[:, first + c * HD : first + (c + 1) * HD] = total
    outs = [
        pltpu.make_async_copy(placed.at[:, pl.ds(0, kw)], kg_out, s_out.at[2, 0]),
        pltpu.make_async_copy(placed.at[:, pl.ds(kw, kw)], vg_out, s_out.at[3, 0]),
    ]
    for copy in outs:
        copy.start()
    for into, out in moves:
        into.wait()
        out.start()
        outs.append(out)
    for copy in outs:
        copy.wait()


def body(queries, keys, values, out_grad, hidden_in, q_weight, lengths, kv_order):
    nr, nc, nro = lax.axis_size("row"), lax.axis_size("col"), lax.axis_size("rollout")
    td, group = queries.shape[0], nr * nc
    length = td * group
    tb, width = hidden_in.shape
    fp = q_weight.shape[0]
    fb = fp // nro
    nj = min(CHUNKS, width // 128)
    dj = width // nj
    nh = -(-(2 * (length // ROLLS) - 1) // td)
    kw = KV * HD
    bf, f32, dma = jnp.bfloat16, jnp.float32, pltpu.SemaphoreType.DMA
    hbm, smem, vmem = (pl.BlockSpec(memory_space=m) for m in (pl.ANY, pltpu.SMEM, pltpu.VMEM))
    call = pl.pallas_call(
        functools.partial(step_kernel, (nc, nr, td, tb, fp, fb, dj, nh, nj)),
        out_shape=(
            jax.ShapeDtypeStruct((td, 2 * kw), f32),
            jax.ShapeDtypeStruct((tb, width), bf),
            jax.ShapeDtypeStruct((fb, width), f32),
        ),
        in_specs=[smem, smem] + [hbm] * 6,
        out_specs=(vmem, hbm, hbm),
        scratch_shapes=[
            pltpu.VMEM((td, HQ * HD), bf),
            pltpu.VMEM((td, HQ * HD), bf),
            pltpu.VMEM(((nh + 1) * td, kw), bf),
            pltpu.VMEM(((nh + 1) * td, kw), bf),
            pltpu.VMEM((td, (nh + 1) * td), f32),
            pltpu.VMEM((td, 1), f32),
            pltpu.VMEM((nc, td, (nc - 1) * fb), bf),
            pltpu.VMEM((length, fp), bf),
            pltpu.VMEM((length, (nc - 1) * fb), bf),
            pltpu.VMEM((nc * fb, length), bf),
            pltpu.VMEM((nj, length, dj), bf),
            pltpu.VMEM((nj, fp, dj), bf),
            pltpu.VMEM((2, nc - 1, nj, tb, dj), bf),
            pltpu.VMEM((2, nj, fb, dj), bf),
            pltpu.VMEM((2, nj, fb, dj), bf),
            pltpu.VMEM((nj, fb, dj), bf),
            pltpu.VMEM((nj, fb, dj), bf),
            pltpu.VMEM((nj, fb, dj), f32),
            pltpu.VMEM(((nh + 1) * td, 2 * kw), f32),
            pltpu.VMEM((nh, td, 2 * kw), bf),
            pltpu.VMEM((nh, td, 2 * kw), bf),
            dma((9,)),
            dma((nh, 2)), dma((nh, 2)),
            dma((2, nc - 1)), dma((2, nc - 1, nj)),
            dma((nc,)), dma((group,)), dma((nc, nr)),
            dma((nc,)), dma((group,)), dma((nc, nr)),
            dma((2, nc - 1)), dma((2, nc - 1, nj)),
            dma((2,)), dma((2, nj)), dma((1,)), dma((nj,)),
            dma((nh,)), dma((nh,)), dma((1,)), dma((2,)),
        ],
        compiler_params=pltpu.CompilerParams(
            collective_id=0, has_side_effects=True, vmem_limit_bytes=67043328
        ),
        name="step",
    )
    kv, ig, wg = call(kv_order, lengths, queries, keys, values, out_grad, hidden_in, q_weight)
    place = pl.pallas_call(
        place_kernel,
        out_shape=(
            jax.ShapeDtypeStruct((td, kw), f32),
            jax.ShapeDtypeStruct((td, kw), f32),
            jax.ShapeDtypeStruct((tb, width), bf),
            jax.ShapeDtypeStruct((fb, width), f32),
        ),
        in_specs=[smem] + [hbm] * 3,
        out_specs=(hbm,) * 4,
        scratch_shapes=[
            pltpu.VMEM((td, 2 * kw), f32),
            pltpu.VMEM((td, 2 * kw), f32),
            pltpu.VMEM((tb, width), bf),
            pltpu.VMEM((fb, width), f32),
            dma((3, PIECES)), dma((4, PIECES)),
        ],
        name="place",
    )
    return place(kv_order, kv, ig, wg)


def solution(mesh):
    return jax.shard_map(
        body,
        mesh=mesh,
        in_specs=(
            P(("rollout", "row", "col"), None),
            P(("rollout", "row", "col"), None),
            P(("rollout", "row", "col"), None),
            P(("rollout", "row", "col"), None),
            P(("rollout", "col"), "row"),
            P("col", "row"),
            P("rollout", None),
            P(),
        ),
        out_specs=(
            P(("rollout", "row", "col"), None),
            P(("rollout", "row", "col"), None),
            P(("rollout", "col"), "row"),
            P(("rollout", "col"), "row"),
        ),
        check_vma=False,
    )
```

```python
import functools
import math

import jax
import jax.numpy as jnp
from jax import lax
from jax.experimental import pallas as pl
from jax.experimental.pallas import tpu as pltpu
from jax.sharding import PartitionSpec as P

HQ = 32
KV = 4
HD = 128
ROLLS = 16
CHUNKS = 8
PIECES = 8
EARLY = 4
MORE = 6
FIRST = 2
LEAD1 = 2
LEAD2 = 1
MESH = pl.DeviceIdType.MESH


def dot32(a, b):
    return jnp.dot(a, b, preferred_element_type=jnp.float32)


def dot_nt(a, b):
    return lax.dot_general(a, b, (((1,), (1,)), ((), ())), preferred_element_type=jnp.float32)


def dot_tn(a, b):
    return lax.dot_general(a, b, (((0,), (0,)), ((), ())), preferred_element_type=jnp.float32)


def step_kernel(
    sizes,
    order_ref, lengths_ref, q_hbm, k_hbm, v_hbm, g_hbm, h_hbm, w_hbm,
    kv_ref, ig_hbm, wg_hbm,
    qv, gv, kb, vb, bias, resp, dq2, a1, a2, a2t, hid, wv, rs, w1s, w1r, w2s, w2r, wo, dka, dks, dkr,
    s_in, s_halo, r_halo, s_g, r_g, s_q1, r_q1, s_f1, s_q2, r_q2, s_f2, s_f3, s_rs, r_rs, s_w1, r_w1, s_w2, r_w2, s_dk, r_dk, s_ig, s_wo,
):
    nc, nr, td, tb, fp, fb, dj, nh, nj = sizes
    early, first, lead1, lead2 = (max(1, x * nj // CHUNKS) for x in (EARLY, FIRST, LEAD1, LEAD2))
    z, row, ro = lax.axis_index("col"), lax.axis_index("row"), lax.axis_index("rollout")
    dev = row * nc + z
    group = nr * nc
    kw = KV * HD
    scale = 1.0 / math.sqrt(HD)
    core, yside = ro ^ 1, ro ^ 2

    def at(d):
        return {"row": d // nc, "col": d % nc}

    own = pl.ds(nh * td, td)
    loads = [
        pltpu.make_async_copy(k_hbm, kb.at[own, :], s_in.at[0]),
        pltpu.make_async_copy(v_hbm, vb.at[own, :], s_in.at[1]),
        pltpu.make_async_copy(q_hbm, qv, s_in.at[2]),
        pltpu.make_async_copy(g_hbm, gv, s_in.at[3]),
    ]
    own_rows = pl.ds(pl.multiple_of(z * tb, tb), tb)
    for j in range(nj):
        loads.append(pltpu.make_async_copy(h_hbm.at[:, pl.ds(j * dj, dj)], hid.at[j, own_rows, :], s_in.at[4]))
        loads.append(pltpu.make_async_copy(w_hbm.at[:, pl.ds(j * dj, dj)], wv.at[j], s_in.at[5 + j * 4 // nj]))
    for copy in loads:
        copy.start()

    barrier = pltpu.get_barrier_semaphore()
    for c in range(1, nc):
        pl.semaphore_signal(barrier, inc=1, device_id={"col": (z + c) % nc}, device_id_type=MESH)
    for r in range(1, nr):
        pl.semaphore_signal(barrier, inc=1, device_id={"row": (row + r) % nr}, device_id_type=MESH)
    pl.semaphore_signal(barrier, inc=1, device_id={"rollout": core}, device_id_type=MESH)
    pl.semaphore_signal(barrier, inc=1, device_id={"rollout": yside}, device_id_type=MESH)
    for h in range(1, nh + 1):
        @pl.when(dev >= h)
        def _(h=h):
            pl.semaphore_signal(barrier, inc=1, device_id=at(dev - h), device_id_type=MESH)

        @pl.when(dev + h < group)
        def _(h=h):
            pl.semaphore_signal(barrier, inc=1, device_id=at(dev + h), device_id_type=MESH)
    peers = nc - 1 + nr - 1 + 2
    for h in range(1, nh + 1):
        peers = peers + jnp.where(dev >= h, 1, 0) + jnp.where(dev + h < group, 1, 0)
    pl.semaphore_wait(barrier, peers)

    def halo(h, i):
        src, dst = ((k_hbm, kb), (v_hbm, vb))[i]
        return pltpu.make_async_remote_copy(
            src_ref=src, dst_ref=dst.at[pl.ds((nh - h) * td, td), :],
            send_sem=s_halo.at[h - 1, i], recv_sem=r_halo.at[h - 1, i],
            device_id=at(lax.rem(dev + h, group)), device_id_type=MESH,
        )

    for h in range(1, nh + 1):
        @pl.when(dev + h < group)
        def _(h=h):
            halo(h, 0).start()
            halo(h, 1).start()

    def plane_rows(p):
        return pl.ds(pl.multiple_of(p * tb, tb), tb)

    def gather(up, hop, j):
        plane = z - (hop - 1) if up else z + (hop - 1)
        src = h_hbm.at[:, pl.ds(pl.multiple_of(j * dj, dj), dj)] if hop == 1 else hid.at[j, plane_rows(plane), :]
        return pltpu.make_async_remote_copy(
            src_ref=src, dst_ref=hid.at[j, plane_rows(plane), :],
            send_sem=s_g.at[0 if up else 1, hop - 1], recv_sem=r_g.at[0 if up else 1, hop - 1, j],
            device_id={"col": z + 1 if up else z - 1}, device_id_type=MESH,
        )

    def gather_sends(up, hop):
        return (z < nc - 1) & (z >= hop - 1) if up else (z > 0) & (z + hop - 1 < nc)

    def gather_lands(up, hop):
        return z >= hop if up else z + hop < nc

    def gather_start(hop, j):
        for up in (True, False):
            @pl.when(gather_sends(up, hop))
            def _(up=up):
                gather(up, hop, j).start()

    def gather_wait(hop, j, relays):
        for up in (True, False):
            on = gather_sends(up, hop + 1) if hop < nc - 1 else jnp.bool_(False)
            on = on if relays else jnp.logical_not(on)

            @pl.when(gather_lands(up, hop) & on)
            def _(up=up):
                plane = z - hop if up else z + hop
                pltpu.make_async_remote_copy(
                    src_ref=hid.at[j, plane_rows(plane), :], dst_ref=hid.at[j, plane_rows(plane), :],
                    send_sem=s_g.at[0 if up else 1, hop - 1], recv_sem=r_g.at[0 if up else 1, hop - 1, j],
                    device_id={"col": z}, device_id_type=MESH,
                ).wait_recv()

    for j in range(first):
        gather_start(1, j)

    pos = dev * td + lax.broadcasted_iota(jnp.int32, (td, 1), 0)
    bound, parts, start = jnp.int32(0), jnp.zeros((td, 1), jnp.int32), jnp.zeros((td, 1), jnp.int32)
    for i in range(2 * ROLLS):
        bound = bound + lengths_ref[0, i]
        reached = pos >= bound
        parts = parts + reached.astype(jnp.int32)
        if i % 2:
            start = jnp.where(reached, bound, start)
    resp[...] = (parts % 2).astype(jnp.float32)
    shape = (td, (nh + 1) * td)
    col = lax.broadcasted_iota(jnp.int32, shape, 1) + (dev - nh) * td
    line = lax.broadcasted_iota(jnp.int32, shape, 0) + dev * td
    bias[...] = jnp.where((col <= line) & (col >= start), 0.0, -jnp.inf)

    for h in range(1, nh + 1):
        rows = pl.ds((nh - h) * td, td)

        @pl.when(dev < h)
        def _(rows=rows):
            kb[rows, :] = jnp.zeros((td, kw), kb.dtype)
            vb[rows, :] = jnp.zeros((td, kw), vb.dtype)

        @pl.when(dev >= h)
        def _(h=h):
            halo(h, 0).wait_recv()
            halo(h, 1).wait_recv()
    for copy in loads[:4]:
        copy.wait()

    per = HQ // KV

    def send_q1(p):
        return pltpu.make_async_remote_copy(
            src_ref=qv.at[:, pl.ds(pl.multiple_of(p * fp, fp), fp)],
            dst_ref=a1.at[pl.ds(pl.multiple_of(dev * td, td), td), :],
            send_sem=s_q1.at[p], recv_sem=r_q1.at[dev],
            device_id={"col": p}, device_id_type=MESH,
        )

    def nth(i):
        return jnp.where(z < nc // 2, KV - 1 - i, i)

    def block(i, _):
        m = jnp.where(i == KV - 1, z, jnp.where(nth(i) == z, nth(KV - 1), nth(i))) if nc == KV else i
        reads = jnp.full((1, HD), order_ref[m], jnp.int32)
        k = jnp.zeros(((nh + 1) * td, HD), jnp.float32)
        v = jnp.zeros(((nh + 1) * td, HD), jnp.float32)
        for c in range(KV):
            k = jnp.where(reads == c, kb[:, c * HD : (c + 1) * HD].astype(jnp.float32), k)
            v = jnp.where(reads == c, vb[:, c * HD : (c + 1) * HD].astype(jnp.float32), v)
        k, v = k.astype(jnp.bfloat16), v.astype(jnp.bfloat16)
        dk = jnp.zeros(((nh + 1) * td, HD), jnp.float32)
        dv = jnp.zeros(((nh + 1) * td, HD), jnp.float32)
        columns = [pl.ds(pl.multiple_of((m * per + hh) * HD, HD), HD) for hh in range(per)]
        qs = [qv[:, cols] for cols in columns]
        gs = [(gv[:, cols].astype(jnp.float32) * resp[...]).astype(jnp.bfloat16) for cols in columns]
        q, g = jnp.concatenate(qs, axis=0), jnp.concatenate(gs, axis=0)
        mask = jnp.concatenate([bias[...]] * per, axis=0)
        s = dot_nt(q, k) * scale + mask
        e = jnp.exp(s - jnp.max(s, axis=1, keepdims=True))
        p = e * (1.0 / jnp.sum(e, axis=1, keepdims=True))
        dp = dot_nt(g, v)
        delta = jnp.sum(p * dp, axis=1, keepdims=True)
        ds = (p * (dp - delta) * scale).astype(jnp.bfloat16)
        new = dot32(ds, k).astype(jnp.bfloat16)
        dqs = [new[hh * td : (hh + 1) * td] for hh in range(per)]
        dk = dot_tn(ds, q)
        dv = dot_tn(p.astype(jnp.bfloat16), g)
        for cols, new in zip(columns, dqs):
            qv[:, cols] = new
        dka[:, pl.ds(pl.multiple_of(m * HD, HD), HD)] = dk
        dka[:, pl.ds(pl.multiple_of(kw + m * HD, HD), HD)] = dv
        if nc == KV:
            @pl.when(m != z)
            def _():
                send_q1(m).start()
        return 0

    lax.fori_loop(0, KV, block, 0)
    if nc != KV:
        for c in range(1, nc):
            send_q1((z + c) % nc).start()

    for p in range(nc):
        for b in range(1, nc):
            o = (p + b) % nc
            dq2[p, :, (b - 1) * fb : b * fb] = qv[:, o * fp + p * fb : o * fp + (p + 1) * fb]

    paired = nc == 4

    def send_q2(p):
        rows = pl.ds(pl.multiple_of(dev * td, td), td)
        return pltpu.make_async_remote_copy(
            src_ref=dq2.at[p], dst_ref=a2.at[rows, :], send_sem=s_q2.at[p], recv_sem=r_q2.at[dev],
            device_id={"col": p}, device_id_type=MESH,
        )

    def send_q2_part(p):
        rows = pl.ds(pl.multiple_of(dev * td, td), td)
        kept = pl.ds(pl.multiple_of((1 - p % 2) * fb, fb), 2 * fb)
        return pltpu.make_async_remote_copy(
            src_ref=dq2.at[p, :, kept], dst_ref=a2.at[rows, kept], send_sem=s_q2.at[p], recv_sem=r_q2.at[dev],
            device_id={"col": p}, device_id_type=MESH,
        )

    def each_q2(act):
        for c in range(1, nc):
            p = (z + c) % nc
            if not paired:
                act(send_q2(p))
                continue

            @pl.when(p // 2 == z // 2)
            def _(p=p):
                act(send_q2(p))

            @pl.when(p // 2 != z // 2)
            def _(p=p):
                act(send_q2_part(p))

    def hand_on(d):
        sibling = z ^ 1
        rows = pl.ds(pl.multiple_of(d * td, td), td)
        return pltpu.make_async_remote_copy(
            src_ref=a1.at[rows, pl.ds(pl.multiple_of(sibling * fb, fb), fb)],
            dst_ref=a2.at[rows, pl.ds(pl.multiple_of((sibling % 2) * 2 * fb, fb), fb)],
            send_sem=s_f3.at[d % nc], recv_sem=r_q2.at[d],
            device_id={"col": sibling}, device_id_type=MESH,
        )

    for j in range(first, early):
        gather_start(1, j)
    inner = (z > 0) & (z < nc - 1)

    def send_second():
        each_q2(lambda copy: copy.start())

    def dk_copy(h):
        return pltpu.make_async_remote_copy(
            src_ref=dks.at[h - 1], dst_ref=dkr.at[h - 1], send_sem=s_dk.at[h - 1], recv_sem=r_dk.at[h - 1],
            device_id=at(lax.rem(dev - h + group, group)), device_id_type=MESH,
        )

    for h in range(1, nh + 1):
        dks[h - 1] = dka[(nh - h) * td : (nh - h + 1) * td, :].astype(jnp.bfloat16)

        @pl.when(dev >= h)
        def _(h=h):
            dk_copy(h).start()

    def piece(d):
        return pl.ds(pl.multiple_of(d * td, td), td)

    def over1(d, r):
        return pltpu.make_async_remote_copy(
            src_ref=a1.at[piece(d), :], dst_ref=a1.at[piece(d), :], send_sem=s_f1.at[d % nc, r], recv_sem=r_q1.at[d],
            device_id={"row": (row + r) % nr}, device_id_type=MESH,
        )

    def over2(d, r):
        return pltpu.make_async_remote_copy(
            src_ref=a2.at[piece(d), :], dst_ref=a2.at[piece(d), :],
            send_sem=s_f2.at[d % nc, r], recv_sem=r_q2.at[d],
            device_id={"row": (row + r) % nr}, device_id_type=MESH,
        )

    def spread(over):
        for r in range(1, nr):
            over(dev, r).start()
        for c in (2, -2, 3, -3, 1, -1) if nc == 4 else range(1, nc):
            other = z + c if nc == 4 else (z + c) % nc

            @pl.when((other >= 0) & (other < nc))
            def _(other=other):
                d = row * nc + other
                over(d, 0).wait_recv()
                for r in range(1, nr):
                    over(d, r).start()
                if over is over1 and paired:
                    @pl.when(other // 2 != z // 2)
                    def _():
                        hand_on(d).start()

    def landed(over):
        for r in range(1, nr):
            for c in range(nc):
                over(((row + r) % nr) * nc + c, 0).wait_recv()

    a1[piece(dev), :] = qv[:, pl.ds(pl.multiple_of(z * fp, fp), fp)]
    a2[piece(dev), :] = dq2[z]
    spread(over1)

    more = max(1, MORE * nj // CHUNKS)

    @pl.when(inner)
    def _():
        send_second()
        for j in range(early, more):
            gather_start(1, j)

    landed(over1)

    def second_map():
        landed(over2)
        for r in range(group * td // tb):
            rows = slice(r * tb, (r + 1) * tb)
            a2t[0:fb, rows] = a1[rows, pl.ds(pl.multiple_of(z * fb, fb), fb)].T
            a2t[fb:, rows] = a2[rows, :].T

    def slot(up, t):
        return jnp.where(up == 0, t - 1, t)

    def rs_copy(way, t, j):
        at_slot = rs.at[way, slot(way, t), j]
        return pltpu.make_async_remote_copy(
            src_ref=at_slot, dst_ref=at_slot, send_sem=s_rs.at[way, slot(way, t)], recv_sem=r_rs.at[way, slot(way, t), j],
            device_id={"col": jnp.where(way == 0, z + 1, z - 1)}, device_id_type=MESH,
        )

    def term(t, j):
        return dot32(a1[plane_rows(t), :], wv[j])

    def rs_sends(j, first, last):
        def one(i, _):
            way = (i + z // (nc // 2)) % 2
            t = jnp.where(way == 0, nc - 1 - i // 2, i // 2)
            lands = jnp.where(way == 0, z > 0, z < nc - 1)
            sends = jnp.where(way == 0, t > z, t < z)

            @pl.when(sends)
            def _():
                part = term(t, j)

                @pl.when(lands)
                def _():
                    rs_copy(way, t, j).wait_recv()
                    rs[way, slot(way, t), j] = (part + rs[way, slot(way, t), j].astype(jnp.float32)).astype(jnp.bfloat16)

                @pl.when(jnp.logical_not(lands))
                def _():
                    rs[way, slot(way, t), j] = part.astype(jnp.bfloat16)

                rs_copy(way, t, j).start()
            return 0

        lax.fori_loop(first, last, one, 0)

    way_z, slot_z = jnp.where(z > 0, 0, 1), jnp.where(z > 0, z - 1, 0)

    def ig_copy(j):
        return pltpu.make_async_copy(
            rs.at[way_z, slot_z, j], ig_hbm.at[:, pl.ds(pl.multiple_of(j * dj, dj), dj)], s_ig.at[0]
        )

    def rs_final(j):
        part = term(z, j)

        @pl.when(z > 0)
        def _():
            rs_copy(0, z, j).wait_recv()

        @pl.when(z < nc - 1)
        def _():
            rs_copy(1, z, j).wait_recv()

        first = part + rs[way_z, slot_z, j].astype(jnp.float32)

        @pl.when((z > 0) & (z < nc - 1))
        def _():
            rs[0, z - 1, j] = (first + rs[1, z, j].astype(jnp.float32)).astype(jnp.bfloat16)

        @pl.when((z == 0) | (z == nc - 1))
        def _():
            rs[way_z, slot_z, j] = first.astype(jnp.bfloat16)

        ig_copy(j).start()

    def wterm(o, j):
        b = lax.rem(o - z + nc, nc)
        return dot32(a2t[pl.ds(pl.multiple_of(b * fb, fb), fb), :], hid[j])

    def w1_copy(i, j):
        return pltpu.make_async_remote_copy(
            src_ref=w1s.at[i, j], dst_ref=w1r.at[i, j], send_sem=s_w1.at[i], recv_sem=r_w1.at[i, j],
            device_id={"rollout": core}, device_id_type=MESH,
        )

    def w2_copy(j):
        return pltpu.make_async_remote_copy(
            src_ref=w2s.at[j], dst_ref=w2r.at[j], send_sem=s_w2.at[0], recv_sem=r_w2.at[j],
            device_id={"rollout": yside}, device_id_type=MESH,
        )

    def wo_copy(j):
        return pltpu.make_async_copy(wo.at[j], wg_hbm.at[:, pl.ds(pl.multiple_of(j * dj, dj), dj)], s_wo.at[j * 2 // nj])

    def weight1(j):
        for hop in range(1, nc):
            gather_wait(hop, j, False)

        def one(i, _):
            w1s[i, j] = wterm(core ^ (2 * i), j).astype(jnp.bfloat16)
            w1_copy(i, j).start()
            return 0

        lax.fori_loop(0, 2, one, 0)

    def weight2(j):
        part = wterm(yside, j)
        w1_copy(1, j).wait_recv()
        w2s[j] = (part + w1r[1, j].astype(jnp.float32)).astype(jnp.bfloat16)
        w2_copy(j).start()

    def weight3(j):
        part = wterm(ro, j)
        w1_copy(0, j).wait_recv()
        w2_copy(j).wait_recv()
        wo[j] = part + w1r[0, j].astype(jnp.float32) + w2r[j].astype(jnp.float32)
        wo_copy(j).start()

    def relay(hop, j):
        gather_wait(hop, j, True)
        gather_start(hop + 1, j)

    pltpu.make_async_copy(hid.at[:, own_rows, :], hid.at[:, own_rows, :], s_in.at[4]).wait()
    for i in range(4):
        quarter = wv.at[pl.ds(i * nj // 4, nj // 4)]
        pltpu.make_async_copy(quarter, quarter, s_in.at[5 + i]).wait()
    for j in range(lead1):
        relay(1, j)

    def step(j, _):
        @pl.when(j < nj - lead1)
        def _():
            relay(1, j + lead1)

        begun = j + jnp.where(inner, more, early)

        @pl.when(begun < nj)
        def _():
            gather_start(1, begun)

        for hop in range(2, nc - 1):
            @pl.when((j > 0) & (j < nj - lead2))
            def _(hop=hop):
                relay(hop, j + lead2)

        @pl.when(j < nj)
        def _():
            rs_sends(j, 0, 2)

        for hop in range(2, nc - 1):
            @pl.when(j == 0)
            def _(hop=hop):
                for i in range(lead2 + 1):
                    relay(hop, i)

        @pl.when(j < nj)
        def _():
            rs_sends(j, 2, 2 * (nc - 1))

        @pl.when(j == 0)
        def _():
            @pl.when(jnp.logical_not(inner))
            def _():
                send_second()

            spread(over2)

        @pl.when(j == 1)
        def _():
            second_map()

        @pl.when(inner & (j == 1))
        def _():
            weight1(0)
            weight1(1)
            weight2(0)

        ahead = j + jnp.where(inner, 1, -1)

        @pl.when((ahead >= jnp.where(inner, 2, 1)) & (ahead <= nj))
        def _():
            weight2(ahead - 1)

        @pl.when((j >= 1) & (ahead < nj))
        def _():
            weight1(ahead)

        @pl.when(j >= 3)
        def _():
            rs_final(j - 3)

        behind = j - jnp.where(inner, 2, 3)

        @pl.when((behind >= 0) & (behind < nj))
        def _():
            weight3(behind)
        return 0

    lax.fori_loop(0, nj + 3, step, 0)

    for h in range(1, nh + 1):
        @pl.when(dev + h < group)
        def _(h=h):
            dk_copy(h).wait_recv()
            dka[pl.ds(nh * td, td), :] = dka[pl.ds(nh * td, td), :] + dkr[h - 1].astype(jnp.float32)
    kv_ref[...] = dka[pl.ds(nh * td, td), :]

    for h in range(1, nh + 1):
        @pl.when(dev + h < group)
        def _(h=h):
            halo(h, 0).wait_send()
            halo(h, 1).wait_send()

        @pl.when(dev >= h)
        def _(h=h):
            dk_copy(h).wait_send()
    for c in range(1, nc):
        send_q1((z + c) % nc).wait_send()
        if paired:
            @pl.when((z + c) % nc // 2 != z // 2)
            def _(c=c):
                hand_on(row * nc + (z + c) % nc).wait_send()
    each_q2(lambda copy: copy.wait_send())
    for over in (over1, over2):
        for r in range(1, nr):
            for c in range(nc):
                over(row * nc + c, r).wait_send()

    def sent(ref, sem):
        pltpu.make_async_copy(ref, ref, sem).wait()

    for hop in range(1, nc):
        for up in (True, False):
            @pl.when(gather_sends(up, hop))
            def _(hop=hop, up=up):
                sent(hid.at[:, own_rows, :], s_g.at[0 if up else 1, hop - 1])
    for way in range(2):
        for t in range(way == 0, nc - way):
            @pl.when(t > z if way == 0 else t < z)
            def _(way=way, t=t):
                sent(rs.at[0, 0], s_rs.at[way, slot(way, t)])
    for i in range(2):
        sent(w1s.at[i], s_w1.at[i])
    sent(w2s, s_w2.at[0])
    sent(rs.at[0, 0], s_ig.at[0])
    for i in range(2):
        sent(wo.at[pl.ds(i * nj // 2, nj // 2)], s_wo.at[i])


def place_kernel(order_ref, kv_hbm, ig_hbm, wg_hbm, kg_out, vg_out, ig_out, wg_out, kv, placed, ig, wg, s_in, s_out):
    kw = kv.shape[1] // 2
    whole = pltpu.make_async_copy(kv_hbm, kv, s_in.at[0, 0])
    whole.start()
    moves = []
    for p in range(PIECES):
        for i, (src, mid, out) in enumerate(((ig_hbm, ig, ig_out), (wg_hbm, wg, wg_out))):
            rows = pl.ds(p * (mid.shape[0] // PIECES), mid.shape[0] // PIECES)
            into = pltpu.make_async_copy(src.at[rows, :], mid.at[rows, :], s_in.at[1 + i, p])
            into.start()
            moves.append((into, pltpu.make_async_copy(mid.at[rows, :], out.at[rows, :], s_out.at[i, p])))
    for into, out in moves:
        into.wait()
        out.start()
    whole.wait()
    for c in range(KV):
        for first in (0, kw):
            total = jnp.zeros((kv.shape[0], HD), jnp.float32)
            for m in range(KV):
                mine = kv[:, first + m * HD : first + (m + 1) * HD]
                total = jnp.where(jnp.full((1, HD), order_ref[m], jnp.int32) == c, mine, total)
            placed[:, first + c * HD : first + (c + 1) * HD] = total
    outs = [
        pltpu.make_async_copy(placed.at[:, pl.ds(0, kw)], kg_out, s_out.at[2, 0]),
        pltpu.make_async_copy(placed.at[:, pl.ds(kw, kw)], vg_out, s_out.at[3, 0]),
    ]
    for copy in outs:
        copy.start()
    for copy in outs + [out for _, out in moves]:
        copy.wait()


def body(queries, keys, values, out_grad, hidden_in, q_weight, lengths, kv_order):
    nr, nc, nro = lax.axis_size("row"), lax.axis_size("col"), lax.axis_size("rollout")
    td, group = queries.shape[0], nr * nc
    length = td * group
    tb, width = hidden_in.shape
    fp = q_weight.shape[0]
    fb = fp // nro
    nj = min(CHUNKS, width // 128)
    dj = width // nj
    nh = -(-(2 * (length // ROLLS) - 1) // td)
    kw = KV * HD
    bf, f32, dma = jnp.bfloat16, jnp.float32, pltpu.SemaphoreType.DMA
    hbm, smem, vmem = (pl.BlockSpec(memory_space=m) for m in (pl.ANY, pltpu.SMEM, pltpu.VMEM))
    call = pl.pallas_call(
        functools.partial(step_kernel, (nc, nr, td, tb, fp, fb, dj, nh, nj)),
        out_shape=(
            jax.ShapeDtypeStruct((td, 2 * kw), f32),
            jax.ShapeDtypeStruct((tb, width), bf),
            jax.ShapeDtypeStruct((fb, width), f32),
        ),
        in_specs=[smem, smem] + [hbm] * 6,
        out_specs=(vmem, hbm, hbm),
        scratch_shapes=[
            pltpu.VMEM((td, HQ * HD), bf),
            pltpu.VMEM((td, HQ * HD), bf),
            pltpu.VMEM(((nh + 1) * td, kw), bf),
            pltpu.VMEM(((nh + 1) * td, kw), bf),
            pltpu.VMEM((td, (nh + 1) * td), f32),
            pltpu.VMEM((td, 1), f32),
            pltpu.VMEM((nc, td, (nc - 1) * fb), bf),
            pltpu.VMEM((length, fp), bf),
            pltpu.VMEM((length, (nc - 1) * fb), bf),
            pltpu.VMEM((nc * fb, length), bf),
            pltpu.VMEM((nj, length, dj), bf),
            pltpu.VMEM((nj, fp, dj), bf),
            pltpu.VMEM((2, nc - 1, nj, tb, dj), bf),
            pltpu.VMEM((2, nj, fb, dj), bf),
            pltpu.VMEM((2, nj, fb, dj), bf),
            pltpu.VMEM((nj, fb, dj), bf),
            pltpu.VMEM((nj, fb, dj), bf),
            pltpu.VMEM((nj, fb, dj), f32),
            pltpu.VMEM(((nh + 1) * td, 2 * kw), f32),
            pltpu.VMEM((nh, td, 2 * kw), bf),
            pltpu.VMEM((nh, td, 2 * kw), bf),
            dma((9,)),
            dma((nh, 2)), dma((nh, 2)),
            dma((2, nc - 1)), dma((2, nc - 1, nj)),
            dma((nc,)), dma((group,)), dma((nc, nr)),
            dma((nc,)), dma((group,)), dma((nc, nr)), dma((nc,)),
            dma((2, nc - 1)), dma((2, nc - 1, nj)),
            dma((2,)), dma((2, nj)), dma((1,)), dma((nj,)),
            dma((nh,)), dma((nh,)), dma((1,)), dma((2,)),
        ],
        compiler_params=pltpu.CompilerParams(
            collective_id=0, has_side_effects=True, vmem_limit_bytes=67043328
        ),
        name="step",
    )
    kv, ig, wg = call(kv_order, lengths, queries, keys, values, out_grad, hidden_in, q_weight)
    place = pl.pallas_call(
        place_kernel,
        out_shape=(
            jax.ShapeDtypeStruct((td, kw), f32),
            jax.ShapeDtypeStruct((td, kw), f32),
            jax.ShapeDtypeStruct((tb, width), bf),
            jax.ShapeDtypeStruct((fb, width), f32),
        ),
        in_specs=[smem] + [hbm] * 3,
        out_specs=(hbm,) * 4,
        scratch_shapes=[
            pltpu.VMEM((td, 2 * kw), f32),
            pltpu.VMEM((td, 2 * kw), f32),
            pltpu.VMEM((tb, width), bf),
            pltpu.VMEM((fb, width), f32),
            dma((3, PIECES)), dma((4, PIECES)),
        ],
        name="place",
    )
    return place(kv_order, kv, ig, wg)


def solution(mesh):
    return jax.shard_map(
        body,
        mesh=mesh,
        in_specs=(
            P(("rollout", "row", "col"), None),
            P(("rollout", "row", "col"), None),
            P(("rollout", "row", "col"), None),
            P(("rollout", "row", "col"), None),
            P(("rollout", "col"), "row"),
            P("col", "row"),
            P("rollout", None),
            P(),
        ),
        out_specs=(
            P(("rollout", "row", "col"), None),
            P(("rollout", "row", "col"), None),
            P(("rollout", "col"), "row"),
            P(("rollout", "col"), "row"),
        ),
        check_vma=False,
    )
```

```python
import functools
import math

import jax
import jax.numpy as jnp
from jax import lax
from jax.experimental import pallas as pl
from jax.experimental.pallas import tpu as pltpu
from jax.sharding import PartitionSpec as P

HQ = 32
KV = 4
HD = 128
ROLLS = 16
CHUNKS = 8
EARLY = 4
MORE = 5
FIRST = 2
LEAD1 = 2
LEAD2 = 1
MESH = pl.DeviceIdType.MESH


def dot32(a, b):
    return jnp.dot(a, b, preferred_element_type=jnp.float32)


def dot_nt(a, b):
    return lax.dot_general(a, b, (((1,), (1,)), ((), ())), preferred_element_type=jnp.float32)


def dot_tn(a, b):
    return lax.dot_general(a, b, (((0,), (0,)), ((), ())), preferred_element_type=jnp.float32)


def step_kernel(
    sizes,
    order_ref, lengths_ref, q_hbm, k_hbm, v_hbm, g_hbm, h_hbm, w_hbm,
    kv_ref, ig, wo,
    qv, gv, kb, vb, bias, resp, dq2, a1, a2, a2t, hid, wv, rs, w1s, w1r, w2s, w2r, dka, dks, dkr,
    s_in, s_halo, r_halo, s_g, r_g, s_q1, r_q1, s_f1, s_q2, r_q2, s_f2, s_f3, s_rs, r_rs, s_w1, r_w1, s_w2, r_w2, s_dk, r_dk,
):
    nc, nr, td, tb, fp, fb, dj, nh, nj = sizes
    early, first, lead1, lead2 = (max(1, x * nj // CHUNKS) for x in (EARLY, FIRST, LEAD1, LEAD2))
    z, row, ro = lax.axis_index("col"), lax.axis_index("row"), lax.axis_index("rollout")
    dev = row * nc + z
    group = nr * nc
    kw = KV * HD
    scale = 1.0 / math.sqrt(HD)
    core, yside = ro ^ 1, ro ^ 2

    def at(d):
        return {"row": d // nc, "col": d % nc}

    own = pl.ds(nh * td, td)
    loads = [
        pltpu.make_async_copy(k_hbm, kb.at[own, :], s_in.at[0]),
        pltpu.make_async_copy(v_hbm, vb.at[own, :], s_in.at[1]),
        pltpu.make_async_copy(q_hbm, qv, s_in.at[2]),
        pltpu.make_async_copy(g_hbm, gv, s_in.at[3]),
    ]
    own_rows = pl.ds(pl.multiple_of(z * tb, tb), tb)
    for j in range(nj):
        loads.append(pltpu.make_async_copy(h_hbm.at[:, pl.ds(j * dj, dj)], hid.at[j, own_rows, :], s_in.at[4]))
        loads.append(pltpu.make_async_copy(w_hbm.at[:, pl.ds(j * dj, dj)], wv.at[j], s_in.at[5 + j * 4 // nj]))
    for copy in loads:
        copy.start()

    barrier = pltpu.get_barrier_semaphore()
    for c in range(1, nc):
        pl.semaphore_signal(barrier, inc=1, device_id={"col": (z + c) % nc}, device_id_type=MESH)
    for r in range(1, nr):
        pl.semaphore_signal(barrier, inc=1, device_id={"row": (row + r) % nr}, device_id_type=MESH)
    pl.semaphore_signal(barrier, inc=1, device_id={"rollout": core}, device_id_type=MESH)
    pl.semaphore_signal(barrier, inc=1, device_id={"rollout": yside}, device_id_type=MESH)
    for h in range(1, nh + 1):
        @pl.when(dev >= h)
        def _(h=h):
            pl.semaphore_signal(barrier, inc=1, device_id=at(dev - h), device_id_type=MESH)

        @pl.when(dev + h < group)
        def _(h=h):
            pl.semaphore_signal(barrier, inc=1, device_id=at(dev + h), device_id_type=MESH)
    peers = nc - 1 + nr - 1 + 2
    for h in range(1, nh + 1):
        peers = peers + jnp.where(dev >= h, 1, 0) + jnp.where(dev + h < group, 1, 0)
    pl.semaphore_wait(barrier, peers)

    def halo(h, i):
        src, dst = ((k_hbm, kb), (v_hbm, vb))[i]
        return pltpu.make_async_remote_copy(
            src_ref=src, dst_ref=dst.at[pl.ds((nh - h) * td, td), :],
            send_sem=s_halo.at[h - 1, i], recv_sem=r_halo.at[h - 1, i],
            device_id=at(lax.rem(dev + h, group)), device_id_type=MESH,
        )

    for h in range(1, nh + 1):
        @pl.when(dev + h < group)
        def _(h=h):
            halo(h, 0).start()
            halo(h, 1).start()

    def plane_rows(p):
        return pl.ds(pl.multiple_of(p * tb, tb), tb)

    def gather(up, hop, j):
        plane = z - (hop - 1) if up else z + (hop - 1)
        src = h_hbm.at[:, pl.ds(pl.multiple_of(j * dj, dj), dj)] if hop == 1 else hid.at[j, plane_rows(plane), :]
        return pltpu.make_async_remote_copy(
            src_ref=src, dst_ref=hid.at[j, plane_rows(plane), :],
            send_sem=s_g.at[0 if up else 1, hop - 1], recv_sem=r_g.at[0 if up else 1, hop - 1, j],
            device_id={"col": z + 1 if up else z - 1}, device_id_type=MESH,
        )

    def gather_sends(up, hop):
        return (z < nc - 1) & (z >= hop - 1) if up else (z > 0) & (z + hop - 1 < nc)

    def gather_lands(up, hop):
        return z >= hop if up else z + hop < nc

    def gather_start(hop, j):
        for up in (True, False):
            @pl.when(gather_sends(up, hop))
            def _(up=up):
                gather(up, hop, j).start()

    def gather_wait(hop, j, relays):
        for up in (True, False):
            on = gather_sends(up, hop + 1) if hop < nc - 1 else jnp.bool_(False)
            on = on if relays else jnp.logical_not(on)

            @pl.when(gather_lands(up, hop) & on)
            def _(up=up):
                plane = z - hop if up else z + hop
                pltpu.make_async_remote_copy(
                    src_ref=hid.at[j, plane_rows(plane), :], dst_ref=hid.at[j, plane_rows(plane), :],
                    send_sem=s_g.at[0 if up else 1, hop - 1], recv_sem=r_g.at[0 if up else 1, hop - 1, j],
                    device_id={"col": z}, device_id_type=MESH,
                ).wait_recv()

    for j in range(first):
        gather_start(1, j)

    pos = dev * td + lax.broadcasted_iota(jnp.int32, (td, 1), 0)
    bound, parts, start = jnp.int32(0), jnp.zeros((td, 1), jnp.int32), jnp.zeros((td, 1), jnp.int32)
    for i in range(2 * ROLLS):
        bound = bound + lengths_ref[0, i]
        reached = pos >= bound
        parts = parts + reached.astype(jnp.int32)
        if i % 2:
            start = jnp.where(reached, bound, start)
    resp[...] = (parts % 2).astype(jnp.float32)
    shape = (td, (nh + 1) * td)
    col = lax.broadcasted_iota(jnp.int32, shape, 1) + (dev - nh) * td
    line = lax.broadcasted_iota(jnp.int32, shape, 0) + dev * td
    bias[...] = jnp.where((col <= line) & (col >= start), 0.0, -jnp.inf)

    for h in range(1, nh + 1):
        rows = pl.ds((nh - h) * td, td)

        @pl.when(dev < h)
        def _(rows=rows):
            kb[rows, :] = jnp.zeros((td, kw), kb.dtype)
            vb[rows, :] = jnp.zeros((td, kw), vb.dtype)

        @pl.when(dev >= h)
        def _(h=h):
            halo(h, 0).wait_recv()
            halo(h, 1).wait_recv()
    for copy in loads[:4]:
        copy.wait()

    per = HQ // KV

    def send_q1(p):
        return pltpu.make_async_remote_copy(
            src_ref=qv.at[:, pl.ds(pl.multiple_of(p * fp, fp), fp)],
            dst_ref=a1.at[pl.ds(pl.multiple_of(dev * td, td), td), :],
            send_sem=s_q1.at[p], recv_sem=r_q1.at[dev],
            device_id={"col": p}, device_id_type=MESH,
        )

    def nth(i):
        return jnp.where(z < nc // 2, KV - 1 - i, i)

    def block(i, _):
        m = jnp.where(i == KV - 1, z, jnp.where(nth(i) == z, nth(KV - 1), nth(i))) if nc == KV else i
        reads = jnp.full((1, HD), order_ref[m], jnp.int32)
        k = jnp.zeros(((nh + 1) * td, HD), jnp.float32)
        v = jnp.zeros(((nh + 1) * td, HD), jnp.float32)
        for c in range(KV):
            k = jnp.where(reads == c, kb[:, c * HD : (c + 1) * HD].astype(jnp.float32), k)
            v = jnp.where(reads == c, vb[:, c * HD : (c + 1) * HD].astype(jnp.float32), v)
        k, v = k.astype(jnp.bfloat16), v.astype(jnp.bfloat16)
        dk = jnp.zeros(((nh + 1) * td, HD), jnp.float32)
        dv = jnp.zeros(((nh + 1) * td, HD), jnp.float32)
        tall = per
        while tall * (nh + 1) > 2 * per:
            tall //= 2
        mask = jnp.concatenate([bias[...]] * tall, axis=0)
        for low in range(0, per, tall):
            columns = [pl.ds(pl.multiple_of((m * per + hh) * HD, HD), HD) for hh in range(low, low + tall)]
            q = jnp.concatenate([qv[:, cols] for cols in columns], axis=0)
            g = jnp.concatenate(
                [(gv[:, cols].astype(jnp.float32) * resp[...]).astype(jnp.bfloat16) for cols in columns], axis=0
            )
            s = dot_nt(q, k) * scale + mask
            e = jnp.exp(s - jnp.max(s, axis=1, keepdims=True))
            p = e * (1.0 / jnp.sum(e, axis=1, keepdims=True))
            dp = dot_nt(g, v)
            delta = jnp.sum(p * dp, axis=1, keepdims=True)
            ds = (p * (dp - delta) * scale).astype(jnp.bfloat16)
            new = dot32(ds, k).astype(jnp.bfloat16)
            dk = dk + dot_tn(ds, q)
            dv = dv + dot_tn(p.astype(jnp.bfloat16), g)
            for i, cols in enumerate(columns):
                qv[:, cols] = new[i * td : (i + 1) * td]
        dka[:, pl.ds(pl.multiple_of(m * HD, HD), HD)] = dk
        dka[:, pl.ds(pl.multiple_of(kw + m * HD, HD), HD)] = dv
        if nc == KV:
            @pl.when(m != z)
            def _():
                send_q1(m).start()
        return 0

    lax.fori_loop(0, KV, block, 0)
    if nc != KV:
        for c in range(1, nc):
            send_q1((z + c) % nc).start()

    for p in range(nc):
        for b in range(1, nc):
            o = (p + b) % nc
            dq2[p, :, (b - 1) * fb : b * fb] = qv[:, o * fp + p * fb : o * fp + (p + 1) * fb]

    paired = nc == 4

    def send_q2(p):
        rows = pl.ds(pl.multiple_of(dev * td, td), td)
        return pltpu.make_async_remote_copy(
            src_ref=dq2.at[p], dst_ref=a2.at[rows, :], send_sem=s_q2.at[p], recv_sem=r_q2.at[dev],
            device_id={"col": p}, device_id_type=MESH,
        )

    def send_q2_part(p):
        rows = pl.ds(pl.multiple_of(dev * td, td), td)
        kept = pl.ds(pl.multiple_of((1 - p % 2) * fb, fb), 2 * fb)
        return pltpu.make_async_remote_copy(
            src_ref=dq2.at[p, :, kept], dst_ref=a2.at[rows, kept], send_sem=s_q2.at[p], recv_sem=r_q2.at[dev],
            device_id={"col": p}, device_id_type=MESH,
        )

    def each_q2(act):
        for c in range(1, nc):
            p = (z + c) % nc
            if not paired:
                act(send_q2(p))
                continue

            @pl.when(p // 2 == z // 2)
            def _(p=p):
                act(send_q2(p))

            @pl.when(p // 2 != z // 2)
            def _(p=p):
                act(send_q2_part(p))

    def hand_on(d):
        sibling = z ^ 1
        rows = pl.ds(pl.multiple_of(d * td, td), td)
        return pltpu.make_async_remote_copy(
            src_ref=a1.at[rows, pl.ds(pl.multiple_of(sibling * fb, fb), fb)],
            dst_ref=a2.at[rows, pl.ds(pl.multiple_of((sibling % 2) * 2 * fb, fb), fb)],
            send_sem=s_f3.at[d % nc], recv_sem=r_q2.at[d],
            device_id={"col": sibling}, device_id_type=MESH,
        )

    for j in range(first, early):
        gather_start(1, j)
    inner = (z > 0) & (z < nc - 1)

    def send_second():
        each_q2(lambda copy: copy.start())

    def dk_copy(h):
        return pltpu.make_async_remote_copy(
            src_ref=dks.at[h - 1], dst_ref=dkr.at[h - 1], send_sem=s_dk.at[h - 1], recv_sem=r_dk.at[h - 1],
            device_id=at(lax.rem(dev - h + group, group)), device_id_type=MESH,
        )

    for h in range(1, nh + 1):
        dks[h - 1] = dka[(nh - h) * td : (nh - h + 1) * td, :].astype(jnp.bfloat16)

        @pl.when(dev >= h)
        def _(h=h):
            dk_copy(h).start()

    def piece(d):
        return pl.ds(pl.multiple_of(d * td, td), td)

    def over1(d, r):
        return pltpu.make_async_remote_copy(
            src_ref=a1.at[piece(d), :], dst_ref=a1.at[piece(d), :], send_sem=s_f1.at[d % nc, r], recv_sem=r_q1.at[d],
            device_id={"row": (row + r) % nr}, device_id_type=MESH,
        )

    def over2(d, r):
        return pltpu.make_async_remote_copy(
            src_ref=a2.at[piece(d), :], dst_ref=a2.at[piece(d), :],
            send_sem=s_f2.at[d % nc, r], recv_sem=r_q2.at[d],
            device_id={"row": (row + r) % nr}, device_id_type=MESH,
        )

    def spread(over):
        for r in range(1, nr):
            over(dev, r).start()
        for c in (2, -2, 3, -3, 1, -1) if nc == 4 else range(1, nc):
            other = z + c if nc == 4 else (z + c) % nc

            @pl.when((other >= 0) & (other < nc))
            def _(other=other):
                d = row * nc + other
                over(d, 0).wait_recv()
                for r in range(1, nr):
                    over(d, r).start()
                if over is over1 and paired:
                    @pl.when(other // 2 != z // 2)
                    def _():
                        hand_on(d).start()

    def landed(over):
        for r in range(1, nr):
            for c in range(nc):
                over(((row + r) % nr) * nc + c, 0).wait_recv()

    a1[piece(dev), :] = qv[:, pl.ds(pl.multiple_of(z * fp, fp), fp)]
    a2[piece(dev), :] = dq2[z]
    spread(over1)

    more = max(1, MORE * nj // CHUNKS)

    @pl.when(inner)
    def _():
        send_second()
        for j in range(early, more):
            gather_start(1, j)

    landed(over1)

    def second_map():
        landed(over2)
        for r in range(group * td // tb):
            rows = slice(r * tb, (r + 1) * tb)
            a2t[0:fb, rows] = a1[rows, pl.ds(pl.multiple_of(z * fb, fb), fb)].T
            a2t[fb:, rows] = a2[rows, :].T

    def slot(up, t):
        return jnp.where(up == 0, t - 1, t)

    def rs_copy(way, t, j):
        at_slot = rs.at[way, slot(way, t), j]
        return pltpu.make_async_remote_copy(
            src_ref=at_slot, dst_ref=at_slot, send_sem=s_rs.at[way, slot(way, t)], recv_sem=r_rs.at[way, slot(way, t), j],
            device_id={"col": jnp.where(way == 0, z + 1, z - 1)}, device_id_type=MESH,
        )

    def term(t, j):
        return dot32(a1[plane_rows(t), :], wv[j])

    def rs_sends(j, first, last):
        def one(i, _):
            way = (i + z // (nc // 2)) % 2
            t = jnp.where(way == 0, nc - 1 - i // 2, i // 2)
            lands = jnp.where(way == 0, z > 0, z < nc - 1)
            sends = jnp.where(way == 0, t > z, t < z)

            @pl.when(sends)
            def _():
                part = term(t, j)

                @pl.when(lands)
                def _():
                    rs_copy(way, t, j).wait_recv()
                    rs[way, slot(way, t), j] = (part + rs[way, slot(way, t), j].astype(jnp.float32)).astype(jnp.bfloat16)

                @pl.when(jnp.logical_not(lands))
                def _():
                    rs[way, slot(way, t), j] = part.astype(jnp.bfloat16)

                rs_copy(way, t, j).start()
            return 0

        lax.fori_loop(first, last, one, 0)

    way_z, slot_z = jnp.where(z > 0, 0, 1), jnp.where(z > 0, z - 1, 0)

    def rs_final(j):
        part = term(z, j)

        @pl.when(z > 0)
        def _():
            rs_copy(0, z, j).wait_recv()

        @pl.when(z < nc - 1)
        def _():
            rs_copy(1, z, j).wait_recv()

        first = part + rs[way_z, slot_z, j].astype(jnp.float32)

        @pl.when((z > 0) & (z < nc - 1))
        def _():
            ig[j] = (first + rs[1, z, j].astype(jnp.float32)).astype(jnp.bfloat16)

        @pl.when((z == 0) | (z == nc - 1))
        def _():
            ig[j] = first.astype(jnp.bfloat16)

    def wterm(o, j):
        b = lax.rem(o - z + nc, nc)
        return dot32(a2t[pl.ds(pl.multiple_of(b * fb, fb), fb), :], hid[j])

    def w1_copy(i, j):
        return pltpu.make_async_remote_copy(
            src_ref=w1s.at[i, j], dst_ref=w1r.at[i, j], send_sem=s_w1.at[i], recv_sem=r_w1.at[i, j],
            device_id={"rollout": core}, device_id_type=MESH,
        )

    def w2_copy(j):
        return pltpu.make_async_remote_copy(
            src_ref=w2s.at[j], dst_ref=w2r.at[j], send_sem=s_w2.at[0], recv_sem=r_w2.at[j],
            device_id={"rollout": yside}, device_id_type=MESH,
        )

    def weight1(j):
        for hop in range(1, nc):
            gather_wait(hop, j, False)

        def one(i, _):
            w1s[i, j] = wterm(core ^ (2 * i), j).astype(jnp.bfloat16)
            w1_copy(i, j).start()
            return 0

        lax.fori_loop(0, 2, one, 0)

    def weight2(j):
        part = wterm(yside, j)
        w1_copy(1, j).wait_recv()
        w2s[j] = (part + w1r[1, j].astype(jnp.float32)).astype(jnp.bfloat16)
        w2_copy(j).start()

    def weight3(j):
        part = wterm(ro, j)
        w1_copy(0, j).wait_recv()
        w2_copy(j).wait_recv()
        wo[j] = part + w1r[0, j].astype(jnp.float32) + w2r[j].astype(jnp.float32)

    def relay(hop, j):
        gather_wait(hop, j, True)
        gather_start(hop + 1, j)

    pltpu.make_async_copy(hid.at[:, own_rows, :], hid.at[:, own_rows, :], s_in.at[4]).wait()
    for i in range(4):
        quarter = wv.at[pl.ds(i * nj // 4, nj // 4)]
        pltpu.make_async_copy(quarter, quarter, s_in.at[5 + i]).wait()
    for j in range(lead1):
        relay(1, j)

    def step(j, _):
        @pl.when(j < nj - lead1)
        def _():
            relay(1, j + lead1)

        begun = j + jnp.where(inner, more, early)

        @pl.when(begun < nj)
        def _():
            gather_start(1, begun)

        for hop in range(2, nc - 1):
            @pl.when((j > 0) & (j < nj - lead2))
            def _(hop=hop):
                relay(hop, j + lead2)

        @pl.when(j < nj)
        def _():
            rs_sends(j, 0, 2)

        for hop in range(2, nc - 1):
            @pl.when(j == 0)
            def _(hop=hop):
                for i in range(lead2 + 1):
                    relay(hop, i)

        @pl.when(j < nj)
        def _():
            rs_sends(j, 2, 2 * (nc - 1))

        @pl.when(j == 0)
        def _():
            @pl.when(jnp.logical_not(inner))
            def _():
                send_second()

            spread(over2)

        @pl.when(j == 1)
        def _():
            second_map()

        @pl.when(inner & (j == 1))
        def _():
            weight1(0)
            weight1(1)
            weight2(0)

        ahead = j + jnp.where(inner, 1, -1)

        @pl.when((ahead >= jnp.where(inner, 2, 1)) & (ahead <= nj))
        def _():
            weight2(ahead - 1)

        @pl.when((j >= 1) & (ahead < nj))
        def _():
            weight1(ahead)

        @pl.when(j >= 3)
        def _():
            rs_final(j - 3)

        behind = j - jnp.where(inner, 2, 3)

        @pl.when((behind >= 0) & (behind < nj))
        def _():
            weight3(behind)
        return 0

    lax.fori_loop(0, nj + 3, step, 0)

    for h in range(1, nh + 1):
        @pl.when(dev + h < group)
        def _(h=h):
            dk_copy(h).wait_recv()
            dka[pl.ds(nh * td, td), :] = dka[pl.ds(nh * td, td), :] + dkr[h - 1].astype(jnp.float32)
    kv_ref[...] = dka[pl.ds(nh * td, td), :]

    for h in range(1, nh + 1):
        @pl.when(dev + h < group)
        def _(h=h):
            halo(h, 0).wait_send()
            halo(h, 1).wait_send()

        @pl.when(dev >= h)
        def _(h=h):
            dk_copy(h).wait_send()
    for c in range(1, nc):
        send_q1((z + c) % nc).wait_send()
        if paired:
            @pl.when((z + c) % nc // 2 != z // 2)
            def _(c=c):
                hand_on(row * nc + (z + c) % nc).wait_send()
    each_q2(lambda copy: copy.wait_send())
    for over in (over1, over2):
        for r in range(1, nr):
            for c in range(nc):
                over(row * nc + c, r).wait_send()

    def sent(ref, sem):
        pltpu.make_async_copy(ref, ref, sem).wait()

    for hop in range(1, nc):
        for up in (True, False):
            @pl.when(gather_sends(up, hop))
            def _(hop=hop, up=up):
                sent(hid.at[:, own_rows, :], s_g.at[0 if up else 1, hop - 1])
    for way in range(2):
        for t in range(way == 0, nc - way):
            @pl.when(t > z if way == 0 else t < z)
            def _(way=way, t=t):
                sent(rs.at[0, 0], s_rs.at[way, slot(way, t)])
    for i in range(2):
        sent(w1s.at[i], s_w1.at[i])
    sent(w2s, s_w2.at[0])


def place_kernel(order_ref, kv, ig, wo, kg_out, vg_out, ig_out, wg_out, placed, s_out):
    kw = kv.shape[1] // 2
    nj, dj = wo.shape[0], wo.shape[2]
    outs = []
    for i, (chunks, out) in enumerate(((wo, wg_out), (ig, ig_out))):
        for j in range(nj):
            outs.append(pltpu.make_async_copy(chunks.at[j], out.at[:, pl.ds(j * dj, dj)], s_out.at[i, j]))
    for copy in outs:
        copy.start()
    for i, out in enumerate((kg_out, vg_out)):
        for c in range(KV):
            total = jnp.zeros((kv.shape[0], HD), jnp.float32)
            for m in range(KV):
                mine = kv[:, i * kw + m * HD : i * kw + (m + 1) * HD]
                total = jnp.where(jnp.full((1, HD), order_ref[m], jnp.int32) == c, mine, total)
            placed[i, :, c * HD : (c + 1) * HD] = total
        copy = pltpu.make_async_copy(placed.at[i], out, s_out.at[2, i])
        copy.start()
        outs.append(copy)
    for copy in outs:
        copy.wait()


def body(queries, keys, values, out_grad, hidden_in, q_weight, lengths, kv_order):
    nr, nc, nro = lax.axis_size("row"), lax.axis_size("col"), lax.axis_size("rollout")
    td, group = queries.shape[0], nr * nc
    length = td * group
    tb, width = hidden_in.shape
    fp = q_weight.shape[0]
    fb = fp // nro
    nj = min(CHUNKS, width // 128)
    dj = width // nj
    nh = -(-(2 * (length // ROLLS) - 1) // td)
    kw = KV * HD
    bf, f32, dma = jnp.bfloat16, jnp.float32, pltpu.SemaphoreType.DMA
    hbm, smem, vmem = (pl.BlockSpec(memory_space=m) for m in (pl.ANY, pltpu.SMEM, pltpu.VMEM))
    call = pl.pallas_call(
        functools.partial(step_kernel, (nc, nr, td, tb, fp, fb, dj, nh, nj)),
        out_shape=(
            pltpu.VMEM((td, 2 * kw), f32),
            pltpu.VMEM((nj, tb, dj), bf),
            pltpu.VMEM((nj, fb, dj), f32),
        ),
        in_specs=[smem, smem] + [hbm] * 6,
        out_specs=(vmem,) * 3,
        scratch_shapes=[
            pltpu.VMEM((td, HQ * HD), bf),
            pltpu.VMEM((td, HQ * HD), bf),
            pltpu.VMEM(((nh + 1) * td, kw), bf),
            pltpu.VMEM(((nh + 1) * td, kw), bf),
            pltpu.VMEM((td, (nh + 1) * td), f32),
            pltpu.VMEM((td, 1), f32),
            pltpu.VMEM((nc, td, (nc - 1) * fb), bf),
            pltpu.VMEM((length, fp), bf),
            pltpu.VMEM((length, (nc - 1) * fb), bf),
            pltpu.VMEM((nc * fb, length), bf),
            pltpu.VMEM((nj, length, dj), bf),
            pltpu.VMEM((nj, fp, dj), bf),
            pltpu.VMEM((2, nc - 1, nj, tb, dj), bf),
            pltpu.VMEM((2, nj, fb, dj), bf),
            pltpu.VMEM((2, nj, fb, dj), bf),
            pltpu.VMEM((nj, fb, dj), bf),
            pltpu.VMEM((nj, fb, dj), bf),
            pltpu.VMEM(((nh + 1) * td, 2 * kw), f32),
            pltpu.VMEM((nh, td, 2 * kw), bf),
            pltpu.VMEM((nh, td, 2 * kw), bf),
            dma((9,)),
            dma((nh, 2)), dma((nh, 2)),
            dma((2, nc - 1)), dma((2, nc - 1, nj)),
            dma((nc,)), dma((group,)), dma((nc, nr)),
            dma((nc,)), dma((group,)), dma((nc, nr)), dma((nc,)),
            dma((2, nc - 1)), dma((2, nc - 1, nj)),
            dma((2,)), dma((2, nj)), dma((1,)), dma((nj,)),
            dma((nh,)), dma((nh,)),
        ],
        compiler_params=pltpu.CompilerParams(
            collective_id=0, has_side_effects=True, vmem_limit_bytes=67043328 - 4 * fb * width - 2 * tb * width - 8 * td * kw - (1 << 17)
        ),
        name="step",
    )
    kv, ig, wg = call(kv_order, lengths, queries, keys, values, out_grad, hidden_in, q_weight)
    place = pl.pallas_call(
        place_kernel,
        out_shape=(
            jax.ShapeDtypeStruct((td, kw), f32),
            jax.ShapeDtypeStruct((td, kw), f32),
            jax.ShapeDtypeStruct((tb, width), bf),
            jax.ShapeDtypeStruct((fb, width), f32),
        ),
        in_specs=[smem, vmem, vmem, vmem],
        out_specs=(hbm,) * 4,
        scratch_shapes=[pltpu.VMEM((2, td, kw), f32), dma((3, nj))],
        compiler_params=pltpu.CompilerParams(vmem_limit_bytes=1 << 22),
        name="place",
    )
    return place(kv_order, *(pltpu.with_memory_space_constraint(x, pltpu.VMEM) for x in (kv, ig, wg)))


def solution(mesh):
    return jax.shard_map(
        body,
        mesh=mesh,
        in_specs=(
            P(("rollout", "row", "col"), None),
            P(("rollout", "row", "col"), None),
            P(("rollout", "row", "col"), None),
            P(("rollout", "row", "col"), None),
            P(("rollout", "col"), "row"),
            P("col", "row"),
            P("rollout", None),
            P(),
        ),
        out_specs=(
            P(("rollout", "row", "col"), None),
            P(("rollout", "row", "col"), None),
            P(("rollout", "col"), "row"),
            P(("rollout", "col"), "row"),
        ),
        check_vma=False,
    )
```

```python
import functools
import math

import jax
import jax.numpy as jnp
from jax import lax
from jax.experimental import pallas as pl
from jax.experimental.pallas import tpu as pltpu
from jax.sharding import PartitionSpec as P

HQ = 32
KV = 4
HD = 128
ROLLS = 16
CHUNKS = 4
EARLY = 2
MORE = 3
FIRST = 1
LEAD1 = 1
LEAD2 = 1
MESH = pl.DeviceIdType.MESH


def dot32(a, b):
    return jnp.dot(a, b, preferred_element_type=jnp.float32)


def dot_nt(a, b):
    return lax.dot_general(a, b, (((1,), (1,)), ((), ())), preferred_element_type=jnp.float32)


def dot_tn(a, b):
    return lax.dot_general(a, b, (((0,), (0,)), ((), ())), preferred_element_type=jnp.float32)


def step_kernel(
    sizes,
    order_ref, lengths_ref, q_hbm, k_hbm, v_hbm, g_hbm, h_hbm, w_hbm,
    kv_ref, ig, wo,
    qv, gv, kb, vb, bias, resp, dq2, a1, a2, a2t, hid, wv, rs, w1s, w1r, w2s, w2r, dka, dks, dkr,
    s_in, s_halo, r_halo, s_g, r_g, s_q1, r_q1, s_f1, s_q2, r_q2, s_f2, s_f3, s_rs, r_rs, s_w1, r_w1, s_w2, r_w2, s_dk, r_dk,
):
    nc, nr, td, tb, fp, fb, dj, nh, nj = sizes
    early, first, lead1, lead2 = (max(1, x * nj // CHUNKS) for x in (EARLY, FIRST, LEAD1, LEAD2))
    z, row, ro = lax.axis_index("col"), lax.axis_index("row"), lax.axis_index("rollout")
    dev = row * nc + z
    group = nr * nc
    kw = KV * HD
    scale = 1.0 / math.sqrt(HD)
    core, yside = ro ^ 1, ro ^ 2

    def at(d):
        return {"row": d // nc, "col": d % nc}

    own = pl.ds(nh * td, td)
    loads = [
        pltpu.make_async_copy(k_hbm, kb.at[own, :], s_in.at[0]),
        pltpu.make_async_copy(v_hbm, vb.at[own, :], s_in.at[1]),
        pltpu.make_async_copy(q_hbm, qv, s_in.at[2]),
        pltpu.make_async_copy(g_hbm, gv, s_in.at[3]),
    ]
    own_rows = pl.ds(pl.multiple_of(z * tb, tb), tb)
    for j in range(nj):
        loads.append(pltpu.make_async_copy(h_hbm.at[:, pl.ds(j * dj, dj)], hid.at[j, own_rows, :], s_in.at[4]))
        loads.append(pltpu.make_async_copy(w_hbm.at[:, pl.ds(j * dj, dj)], wv.at[j], s_in.at[5 + j * 4 // nj]))
    for copy in loads:
        copy.start()

    barrier = pltpu.get_barrier_semaphore()
    for c in range(1, nc):
        pl.semaphore_signal(barrier, inc=1, device_id={"col": (z + c) % nc}, device_id_type=MESH)
    for r in range(1, nr):
        pl.semaphore_signal(barrier, inc=1, device_id={"row": (row + r) % nr}, device_id_type=MESH)
    pl.semaphore_signal(barrier, inc=1, device_id={"rollout": core}, device_id_type=MESH)
    pl.semaphore_signal(barrier, inc=1, device_id={"rollout": yside}, device_id_type=MESH)
    for h in range(1, nh + 1):
        @pl.when(dev >= h)
        def _(h=h):
            pl.semaphore_signal(barrier, inc=1, device_id=at(dev - h), device_id_type=MESH)

        @pl.when(dev + h < group)
        def _(h=h):
            pl.semaphore_signal(barrier, inc=1, device_id=at(dev + h), device_id_type=MESH)
    peers = nc - 1 + nr - 1 + 2
    for h in range(1, nh + 1):
        peers = peers + jnp.where(dev >= h, 1, 0) + jnp.where(dev + h < group, 1, 0)
    pl.semaphore_wait(barrier, peers)

    def halo(h, i):
        src, dst = ((k_hbm, kb), (v_hbm, vb))[i]
        return pltpu.make_async_remote_copy(
            src_ref=src, dst_ref=dst.at[pl.ds((nh - h) * td, td), :],
            send_sem=s_halo.at[h - 1, i], recv_sem=r_halo.at[h - 1, i],
            device_id=at(lax.rem(dev + h, group)), device_id_type=MESH,
        )

    for h in range(1, nh + 1):
        @pl.when(dev + h < group)
        def _(h=h):
            halo(h, 0).start()
            halo(h, 1).start()

    def plane_rows(p):
        return pl.ds(pl.multiple_of(p * tb, tb), tb)

    def gather(up, hop, j):
        plane = z - (hop - 1) if up else z + (hop - 1)
        src = h_hbm.at[:, pl.ds(pl.multiple_of(j * dj, dj), dj)] if hop == 1 else hid.at[j, plane_rows(plane), :]
        return pltpu.make_async_remote_copy(
            src_ref=src, dst_ref=hid.at[j, plane_rows(plane), :],
            send_sem=s_g.at[0 if up else 1, hop - 1], recv_sem=r_g.at[0 if up else 1, hop - 1, j],
            device_id={"col": z + 1 if up else z - 1}, device_id_type=MESH,
        )

    def gather_sends(up, hop):
        return (z < nc - 1) & (z >= hop - 1) if up else (z > 0) & (z + hop - 1 < nc)

    def gather_lands(up, hop):
        return z >= hop if up else z + hop < nc

    def gather_start(hop, j):
        for up in (True, False):
            @pl.when(gather_sends(up, hop))
            def _(up=up):
                gather(up, hop, j).start()

    def gather_wait(hop, j, relays):
        for up in (True, False):
            on = gather_sends(up, hop + 1) if hop < nc - 1 else jnp.bool_(False)
            on = on if relays else jnp.logical_not(on)

            @pl.when(gather_lands(up, hop) & on)
            def _(up=up):
                plane = z - hop if up else z + hop
                pltpu.make_async_remote_copy(
                    src_ref=hid.at[j, plane_rows(plane), :], dst_ref=hid.at[j, plane_rows(plane), :],
                    send_sem=s_g.at[0 if up else 1, hop - 1], recv_sem=r_g.at[0 if up else 1, hop - 1, j],
                    device_id={"col": z}, device_id_type=MESH,
                ).wait_recv()

    for j in range(first):
        gather_start(1, j)

    pos = dev * td + lax.broadcasted_iota(jnp.int32, (td, 1), 0)
    bound, parts, start = jnp.int32(0), jnp.zeros((td, 1), jnp.int32), jnp.zeros((td, 1), jnp.int32)
    for i in range(2 * ROLLS):
        bound = bound + lengths_ref[0, i]
        reached = pos >= bound
        parts = parts + reached.astype(jnp.int32)
        if i % 2:
            start = jnp.where(reached, bound, start)
    resp[...] = (parts % 2).astype(jnp.float32)
    shape = (td, (nh + 1) * td)
    col = lax.broadcasted_iota(jnp.int32, shape, 1) + (dev - nh) * td
    line = lax.broadcasted_iota(jnp.int32, shape, 0) + dev * td
    bias[...] = jnp.where((col <= line) & (col >= start), 0.0, -jnp.inf)

    for h in range(1, nh + 1):
        rows = pl.ds((nh - h) * td, td)

        @pl.when(dev < h)
        def _(rows=rows):
            kb[rows, :] = jnp.zeros((td, kw), kb.dtype)
            vb[rows, :] = jnp.zeros((td, kw), vb.dtype)

        @pl.when(dev >= h)
        def _(h=h):
            halo(h, 0).wait_recv()
            halo(h, 1).wait_recv()
    for copy in loads[:4]:
        copy.wait()

    per = HQ // KV

    def send_q1(p):
        return pltpu.make_async_remote_copy(
            src_ref=qv.at[:, pl.ds(pl.multiple_of(p * fp, fp), fp)],
            dst_ref=a1.at[pl.ds(pl.multiple_of(dev * td, td), td), :],
            send_sem=s_q1.at[p], recv_sem=r_q1.at[dev],
            device_id={"col": p}, device_id_type=MESH,
        )

    def nth(i):
        return jnp.where(z < nc // 2, KV - 1 - i, i)

    def block(i, _):
        m = jnp.where(i == KV - 1, z, jnp.where(nth(i) == z, nth(KV - 1), nth(i))) if nc == KV else i
        reads = jnp.full((1, HD), order_ref[m], jnp.int32)
        k = jnp.zeros(((nh + 1) * td, HD), jnp.float32)
        v = jnp.zeros(((nh + 1) * td, HD), jnp.float32)
        for c in range(KV):
            k = jnp.where(reads == c, kb[:, c * HD : (c + 1) * HD].astype(jnp.float32), k)
            v = jnp.where(reads == c, vb[:, c * HD : (c + 1) * HD].astype(jnp.float32), v)
        k, v = k.astype(jnp.bfloat16), v.astype(jnp.bfloat16)
        dk = jnp.zeros(((nh + 1) * td, HD), jnp.float32)
        dv = jnp.zeros(((nh + 1) * td, HD), jnp.float32)
        tall = per
        while tall * (nh + 1) > 2 * per:
            tall //= 2
        mask = jnp.concatenate([bias[...]] * tall, axis=0)
        for low in range(0, per, tall):
            columns = [pl.ds(pl.multiple_of((m * per + hh) * HD, HD), HD) for hh in range(low, low + tall)]
            q = jnp.concatenate([qv[:, cols] for cols in columns], axis=0)
            g = jnp.concatenate(
                [(gv[:, cols].astype(jnp.float32) * resp[...]).astype(jnp.bfloat16) for cols in columns], axis=0
            )
            s = dot_nt(q, k) * scale + mask
            e = jnp.exp(s - jnp.max(s, axis=1, keepdims=True))
            p = e * (1.0 / jnp.sum(e, axis=1, keepdims=True))
            dp = dot_nt(g, v)
            delta = jnp.sum(p * dp, axis=1, keepdims=True)
            ds = (p * (dp - delta) * scale).astype(jnp.bfloat16)
            new = dot32(ds, k).astype(jnp.bfloat16)
            dk = dk + dot_tn(ds, q)
            dv = dv + dot_tn(p.astype(jnp.bfloat16), g)
            for i, cols in enumerate(columns):
                qv[:, cols] = new[i * td : (i + 1) * td]
        dka[:, pl.ds(pl.multiple_of(m * HD, HD), HD)] = dk
        dka[:, pl.ds(pl.multiple_of(kw + m * HD, HD), HD)] = dv
        if nc == KV:
            @pl.when(m != z)
            def _():
                send_q1(m).start()
        return 0

    lax.fori_loop(0, KV, block, 0)
    if nc != KV:
        for c in range(1, nc):
            send_q1((z + c) % nc).start()

    for p in range(nc):
        for b in range(1, nc):
            o = (p + b) % nc
            dq2[p, :, (b - 1) * fb : b * fb] = qv[:, o * fp + p * fb : o * fp + (p + 1) * fb]

    paired = nc == 4

    def send_q2(p):
        rows = pl.ds(pl.multiple_of(dev * td, td), td)
        return pltpu.make_async_remote_copy(
            src_ref=dq2.at[p], dst_ref=a2.at[rows, :], send_sem=s_q2.at[p], recv_sem=r_q2.at[dev],
            device_id={"col": p}, device_id_type=MESH,
        )

    def send_q2_part(p):
        rows = pl.ds(pl.multiple_of(dev * td, td), td)
        kept = pl.ds(pl.multiple_of((1 - p % 2) * fb, fb), 2 * fb)
        return pltpu.make_async_remote_copy(
            src_ref=dq2.at[p, :, kept], dst_ref=a2.at[rows, kept], send_sem=s_q2.at[p], recv_sem=r_q2.at[dev],
            device_id={"col": p}, device_id_type=MESH,
        )

    def each_q2(act):
        for c in range(1, nc):
            p = (z + c) % nc
            if not paired:
                act(send_q2(p))
                continue

            @pl.when(p // 2 == z // 2)
            def _(p=p):
                act(send_q2(p))

            @pl.when(p // 2 != z // 2)
            def _(p=p):
                act(send_q2_part(p))

    def hand_on(d):
        sibling = z ^ 1
        rows = pl.ds(pl.multiple_of(d * td, td), td)
        return pltpu.make_async_remote_copy(
            src_ref=a1.at[rows, pl.ds(pl.multiple_of(sibling * fb, fb), fb)],
            dst_ref=a2.at[rows, pl.ds(pl.multiple_of((sibling % 2) * 2 * fb, fb), fb)],
            send_sem=s_f3.at[d % nc], recv_sem=r_q2.at[d],
            device_id={"col": sibling}, device_id_type=MESH,
        )

    for j in range(first, early):
        gather_start(1, j)
    inner = (z > 0) & (z < nc - 1)

    def send_second():
        each_q2(lambda copy: copy.start())

    def dk_copy(h):
        return pltpu.make_async_remote_copy(
            src_ref=dks.at[h - 1], dst_ref=dkr.at[h - 1], send_sem=s_dk.at[h - 1], recv_sem=r_dk.at[h - 1],
            device_id=at(lax.rem(dev - h + group, group)), device_id_type=MESH,
        )

    for h in range(1, nh + 1):
        dks[h - 1] = dka[(nh - h) * td : (nh - h + 1) * td, :].astype(jnp.bfloat16)

        @pl.when(dev >= h)
        def _(h=h):
            dk_copy(h).start()

    def piece(d):
        return pl.ds(pl.multiple_of(d * td, td), td)

    def over1(d, r):
        return pltpu.make_async_remote_copy(
            src_ref=a1.at[piece(d), :], dst_ref=a1.at[piece(d), :], send_sem=s_f1.at[d % nc, r], recv_sem=r_q1.at[d],
            device_id={"row": (row + r) % nr}, device_id_type=MESH,
        )

    def over2(d, r):
        return pltpu.make_async_remote_copy(
            src_ref=a2.at[piece(d), :], dst_ref=a2.at[piece(d), :],
            send_sem=s_f2.at[d % nc, r], recv_sem=r_q2.at[d],
            device_id={"row": (row + r) % nr}, device_id_type=MESH,
        )

    def spread(over):
        for r in range(1, nr):
            over(dev, r).start()
        for c in (2, -2, 3, -3, 1, -1) if nc == 4 else range(1, nc):
            other = z + c if nc == 4 else (z + c) % nc

            @pl.when((other >= 0) & (other < nc))
            def _(other=other):
                d = row * nc + other
                over(d, 0).wait_recv()
                for r in range(1, nr):
                    over(d, r).start()
                if over is over1 and paired:
                    @pl.when(other // 2 != z // 2)
                    def _():
                        hand_on(d).start()

    def landed(over):
        for r in range(1, nr):
            for c in range(nc):
                over(((row + r) % nr) * nc + c, 0).wait_recv()

    a1[piece(dev), :] = qv[:, pl.ds(pl.multiple_of(z * fp, fp), fp)]
    a2[piece(dev), :] = dq2[z]
    spread(over1)

    more = max(1, MORE * nj // CHUNKS)

    @pl.when(inner)
    def _():
        send_second()
        for j in range(early, more):
            gather_start(1, j)

    landed(over1)

    def second_map():
        landed(over2)
        for r in range(group * td // tb):
            rows = slice(r * tb, (r + 1) * tb)
            a2t[0:fb, rows] = a1[rows, pl.ds(pl.multiple_of(z * fb, fb), fb)].T
            a2t[fb:, rows] = a2[rows, :].T

    def slot(up, t):
        return jnp.where(up == 0, t - 1, t)

    half = tb // 2

    def rs_copy(way, t, j, part):
        at_slot = rs.at[way, slot(way, t), j, pl.ds(part * half, half), :]
        return pltpu.make_async_remote_copy(
            src_ref=at_slot, dst_ref=at_slot, send_sem=s_rs.at[way, slot(way, t)], recv_sem=r_rs.at[way, slot(way, t), j, part],
            device_id={"col": jnp.where(way == 0, z + 1, z - 1)}, device_id_type=MESH,
        )

    def term(t, j):
        return dot32(a1[plane_rows(t), :], wv[j])

    def rs_sends(j, first, last):
        def one(i, _):
            way = (i + z // (nc // 2)) % 2
            t = jnp.where(way == 0, nc - 1 - i // 2, i // 2)
            lands = jnp.where(way == 0, z > 0, z < nc - 1)
            sends = jnp.where(way == 0, t > z, t < z)

            @pl.when(sends)
            def _():
                total = term(t, j)
                for part in range(2):
                    rows = pl.ds(part * half, half)
                    mine = total[part * half : (part + 1) * half]

                    @pl.when(lands)
                    def _(part=part, rows=rows, mine=mine):
                        rs_copy(way, t, j, part).wait_recv()
                        rs[way, slot(way, t), j, rows, :] = (
                            mine + rs[way, slot(way, t), j, rows, :].astype(jnp.float32)
                        ).astype(jnp.bfloat16)

                    @pl.when(jnp.logical_not(lands))
                    def _(rows=rows, mine=mine):
                        rs[way, slot(way, t), j, rows, :] = mine.astype(jnp.bfloat16)

                    rs_copy(way, t, j, part).start()
            return 0

        lax.fori_loop(first, last, one, 0)

    way_z, slot_z = jnp.where(z > 0, 0, 1), jnp.where(z > 0, z - 1, 0)

    def rs_final(j):
        part = term(z, j)

        @pl.when(z > 0)
        def _():
            for i in range(2):
                rs_copy(0, z, j, i).wait_recv()

        @pl.when(z < nc - 1)
        def _():
            for i in range(2):
                rs_copy(1, z, j, i).wait_recv()

        first = part + rs[way_z, slot_z, j].astype(jnp.float32)

        @pl.when((z > 0) & (z < nc - 1))
        def _():
            ig[j] = (first + rs[1, z, j].astype(jnp.float32)).astype(jnp.bfloat16)

        @pl.when((z == 0) | (z == nc - 1))
        def _():
            ig[j] = first.astype(jnp.bfloat16)

    def wterm(o, j):
        b = lax.rem(o - z + nc, nc)
        return dot32(a2t[pl.ds(pl.multiple_of(b * fb, fb), fb), :], hid[j])

    def w1_copy(i, j):
        return pltpu.make_async_remote_copy(
            src_ref=w1s.at[i, j], dst_ref=w1r.at[i, j], send_sem=s_w1.at[i], recv_sem=r_w1.at[i, j],
            device_id={"rollout": core}, device_id_type=MESH,
        )

    def w2_copy(j):
        return pltpu.make_async_remote_copy(
            src_ref=w2s.at[j], dst_ref=w2r.at[j], send_sem=s_w2.at[0], recv_sem=r_w2.at[j],
            device_id={"rollout": yside}, device_id_type=MESH,
        )

    def weight1(j):
        for hop in range(1, nc):
            gather_wait(hop, j, False)

        def one(i, _):
            w1s[i, j] = wterm(core ^ (2 * i), j).astype(jnp.bfloat16)
            w1_copy(i, j).start()
            return 0

        lax.fori_loop(0, 2, one, 0)

    def weight2(j):
        part = wterm(yside, j)
        w1_copy(1, j).wait_recv()
        w2s[j] = (part + w1r[1, j].astype(jnp.float32)).astype(jnp.bfloat16)
        w2_copy(j).start()

    def weight3(j):
        part = wterm(ro, j)
        w1_copy(0, j).wait_recv()
        w2_copy(j).wait_recv()
        wo[j] = part + w1r[0, j].astype(jnp.float32) + w2r[j].astype(jnp.float32)

    def relay(hop, j):
        gather_wait(hop, j, True)
        gather_start(hop + 1, j)

    pltpu.make_async_copy(hid.at[:, own_rows, :], hid.at[:, own_rows, :], s_in.at[4]).wait()
    for i in range(4):
        quarter = wv.at[pl.ds(i * nj // 4, nj // 4)]
        pltpu.make_async_copy(quarter, quarter, s_in.at[5 + i]).wait()
    for j in range(lead1):
        relay(1, j)

    def step(j, _):
        @pl.when(j < nj - lead1)
        def _():
            relay(1, j + lead1)

        begun = j + jnp.where(inner, more, early)

        @pl.when(begun < nj)
        def _():
            gather_start(1, begun)

        for hop in range(2, nc - 1):
            @pl.when((j > 0) & (j < nj - lead2))
            def _(hop=hop):
                relay(hop, j + lead2)

        @pl.when(j < nj)
        def _():
            rs_sends(j, 0, 2)

        for hop in range(2, nc - 1):
            @pl.when(j == 0)
            def _(hop=hop):
                for i in range(lead2 + 1):
                    relay(hop, i)

        @pl.when(j < nj)
        def _():
            rs_sends(j, 2, 2 * (nc - 1))

        @pl.when(j == 0)
        def _():
            @pl.when(jnp.logical_not(inner))
            def _():
                send_second()

            spread(over2)

        @pl.when(j == 1)
        def _():
            second_map()

        @pl.when(inner & (j == 1))
        def _():
            weight1(0)
            weight1(1)
            weight2(0)

        ahead = j + jnp.where(inner, 1, -1)

        @pl.when((ahead >= jnp.where(inner, 2, 1)) & (ahead <= nj))
        def _():
            weight2(ahead - 1)

        @pl.when((j >= 1) & (ahead < nj))
        def _():
            weight1(ahead)

        @pl.when(j >= 3)
        def _():
            rs_final(j - 3)

        behind = j - jnp.where(inner, 2, 3)

        @pl.when((behind >= 0) & (behind < nj))
        def _():
            weight3(behind)
        return 0

    lax.fori_loop(0, nj + 3, step, 0)

    for h in range(1, nh + 1):
        @pl.when(dev + h < group)
        def _(h=h):
            dk_copy(h).wait_recv()
            dka[pl.ds(nh * td, td), :] = dka[pl.ds(nh * td, td), :] + dkr[h - 1].astype(jnp.float32)
    kv_ref[...] = dka[pl.ds(nh * td, td), :]

    for h in range(1, nh + 1):
        @pl.when(dev + h < group)
        def _(h=h):
            halo(h, 0).wait_send()
            halo(h, 1).wait_send()

        @pl.when(dev >= h)
        def _(h=h):
            dk_copy(h).wait_send()
    for c in range(1, nc):
        send_q1((z + c) % nc).wait_send()
        if paired:
            @pl.when((z + c) % nc // 2 != z // 2)
            def _(c=c):
                hand_on(row * nc + (z + c) % nc).wait_send()
    each_q2(lambda copy: copy.wait_send())
    for over in (over1, over2):
        for r in range(1, nr):
            for c in range(nc):
                over(row * nc + c, r).wait_send()

    def sent(ref, sem):
        pltpu.make_async_copy(ref, ref, sem).wait()

    for hop in range(1, nc):
        for up in (True, False):
            @pl.when(gather_sends(up, hop))
            def _(hop=hop, up=up):
                sent(hid.at[:, own_rows, :], s_g.at[0 if up else 1, hop - 1])
    for way in range(2):
        for t in range(way == 0, nc - way):
            @pl.when(t > z if way == 0 else t < z)
            def _(way=way, t=t):
                sent(rs.at[0, 0], s_rs.at[way, slot(way, t)])
    for i in range(2):
        sent(w1s.at[i], s_w1.at[i])
    sent(w2s, s_w2.at[0])


def place_kernel(order_ref, kv, ig, wo, kg_out, vg_out, ig_out, wg_out, placed, s_out):
    kw = kv.shape[1] // 2
    nj, dj = wo.shape[0], wo.shape[2]
    outs = []
    for i, (chunks, out) in enumerate(((wo, wg_out), (ig, ig_out))):
        for j in range(nj):
            outs.append(pltpu.make_async_copy(chunks.at[j], out.at[:, pl.ds(j * dj, dj)], s_out.at[i, j]))
    for copy in outs:
        copy.start()
    for i, out in enumerate((kg_out, vg_out)):
        for c in range(KV):
            total = jnp.zeros((kv.shape[0], HD), jnp.float32)
            for m in range(KV):
                mine = kv[:, i * kw + m * HD : i * kw + (m + 1) * HD]
                total = jnp.where(jnp.full((1, HD), order_ref[m], jnp.int32) == c, mine, total)
            placed[i, :, c * HD : (c + 1) * HD] = total
        copy = pltpu.make_async_copy(placed.at[i], out, s_out.at[2, i])
        copy.start()
        outs.append(copy)
    for copy in outs:
        copy.wait()


def body(queries, keys, values, out_grad, hidden_in, q_weight, lengths, kv_order):
    nr, nc, nro = lax.axis_size("row"), lax.axis_size("col"), lax.axis_size("rollout")
    td, group = queries.shape[0], nr * nc
    length = td * group
    tb, width = hidden_in.shape
    fp = q_weight.shape[0]
    fb = fp // nro
    nj = min(CHUNKS, width // 128)
    dj = width // nj
    nh = -(-(2 * (length // ROLLS) - 1) // td)
    kw = KV * HD
    bf, f32, dma = jnp.bfloat16, jnp.float32, pltpu.SemaphoreType.DMA
    hbm, smem, vmem = (pl.BlockSpec(memory_space=m) for m in (pl.ANY, pltpu.SMEM, pltpu.VMEM))
    call = pl.pallas_call(
        functools.partial(step_kernel, (nc, nr, td, tb, fp, fb, dj, nh, nj)),
        out_shape=(
            pltpu.VMEM((td, 2 * kw), f32),
            pltpu.VMEM((nj, tb, dj), bf),
            pltpu.VMEM((nj, fb, dj), f32),
        ),
        in_specs=[smem, smem] + [hbm] * 6,
        out_specs=(vmem,) * 3,
        scratch_shapes=[
            pltpu.VMEM((td, HQ * HD), bf),
            pltpu.VMEM((td, HQ * HD), bf),
            pltpu.VMEM(((nh + 1) * td, kw), bf),
            pltpu.VMEM(((nh + 1) * td, kw), bf),
            pltpu.VMEM((td, (nh + 1) * td), f32),
            pltpu.VMEM((td, 1), f32),
            pltpu.VMEM((nc, td, (nc - 1) * fb), bf),
            pltpu.VMEM((length, fp), bf),
            pltpu.VMEM((length, (nc - 1) * fb), bf),
            pltpu.VMEM((nc * fb, length), bf),
            pltpu.VMEM((nj, length, dj), bf),
            pltpu.VMEM((nj, fp, dj), bf),
            pltpu.VMEM((2, nc - 1, nj, tb, dj), bf),
            pltpu.VMEM((2, nj, fb, dj), bf),
            pltpu.VMEM((2, nj, fb, dj), bf),
            pltpu.VMEM((nj, fb, dj), bf),
            pltpu.VMEM((nj, fb, dj), bf),
            pltpu.VMEM(((nh + 1) * td, 2 * kw), f32),
            pltpu.VMEM((nh, td, 2 * kw), bf),
            pltpu.VMEM((nh, td, 2 * kw), bf),
            dma((9,)),
            dma((nh, 2)), dma((nh, 2)),
            dma((2, nc - 1)), dma((2, nc - 1, nj)),
            dma((nc,)), dma((group,)), dma((nc, nr)),
            dma((nc,)), dma((group,)), dma((nc, nr)), dma((nc,)),
            dma((2, nc - 1)), dma((2, nc - 1, nj, 2)),
            dma((2,)), dma((2, nj)), dma((1,)), dma((nj,)),
            dma((nh,)), dma((nh,)),
        ],
        compiler_params=pltpu.CompilerParams(
            collective_id=0, has_side_effects=True, vmem_limit_bytes=67043328 - 4 * fb * width - 2 * tb * width - 8 * td * kw - (1 << 17)
        ),
        name="step",
    )
    kv, ig, wg = call(kv_order, lengths, queries, keys, values, out_grad, hidden_in, q_weight)
    place = pl.pallas_call(
        place_kernel,
        out_shape=(
            jax.ShapeDtypeStruct((td, kw), f32),
            jax.ShapeDtypeStruct((td, kw), f32),
            jax.ShapeDtypeStruct((tb, width), bf),
            jax.ShapeDtypeStruct((fb, width), f32),
        ),
        in_specs=[smem, vmem, vmem, vmem],
        out_specs=(hbm,) * 4,
        scratch_shapes=[pltpu.VMEM((2, td, kw), f32), dma((3, nj))],
        compiler_params=pltpu.CompilerParams(vmem_limit_bytes=1 << 22),
        name="place",
    )
    return place(kv_order, *(pltpu.with_memory_space_constraint(x, pltpu.VMEM) for x in (kv, ig, wg)))


def solution(mesh):
    return jax.shard_map(
        body,
        mesh=mesh,
        in_specs=(
            P(("rollout", "row", "col"), None),
            P(("rollout", "row", "col"), None),
            P(("rollout", "row", "col"), None),
            P(("rollout", "row", "col"), None),
            P(("rollout", "col"), "row"),
            P("col", "row"),
            P("rollout", None),
            P(),
        ),
        out_specs=(
            P(("rollout", "row", "col"), None),
            P(("rollout", "row", "col"), None),
            P(("rollout", "col"), "row"),
            P(("rollout", "col"), "row"),
        ),
        check_vma=False,
    )
```

```python
import functools
import math

import jax
import jax.numpy as jnp
from jax import lax
from jax.experimental import pallas as pl
from jax.experimental.pallas import tpu as pltpu
from jax.sharding import PartitionSpec as P

HQ = 32
KV = 4
HD = 128
ROLLS = 16
CHUNKS = 4
EARLY = 2
MORE = 3
FIRST = 1
LEAD1 = 1
LEAD2 = 1
MESH = pl.DeviceIdType.MESH


def dot32(a, b):
    return jnp.dot(a, b, preferred_element_type=jnp.float32)


def dot_nt(a, b):
    return lax.dot_general(a, b, (((1,), (1,)), ((), ())), preferred_element_type=jnp.float32)


def dot_tn(a, b):
    return lax.dot_general(a, b, (((0,), (0,)), ((), ())), preferred_element_type=jnp.float32)


def step_kernel(
    sizes,
    order_ref, lengths_ref, q_hbm, k_hbm, v_hbm, g_hbm, h_hbm, w_hbm,
    kv_ref, ig, wo,
    qv, gv, kb, vb, bias, resp, dq2, a1, a2, a2t, hid, wv, rs, w1s, w1r, w2s, w2r, dka, dks, dkr,
    s_in, s_halo, r_halo, s_g, r_g, s_q1, r_q1, s_f1, s_q2, r_q2, s_f2, s_f3, s_rs, r_rs, s_w1, r_w1, s_w2, r_w2, s_dk, r_dk,
):
    nc, nr, td, tb, fp, fb, dj, nh, nj = sizes
    early, first, lead1, lead2 = (max(1, x * nj // CHUNKS) for x in (EARLY, FIRST, LEAD1, LEAD2))
    z, row, ro = lax.axis_index("col"), lax.axis_index("row"), lax.axis_index("rollout")
    dev = row * nc + z
    group = nr * nc
    kw = KV * HD
    scale = 1.0 / math.sqrt(HD)
    core, yside = ro ^ 1, ro ^ 2

    def at(d):
        return {"row": d // nc, "col": d % nc}

    own = pl.ds(nh * td, td)
    loads = [
        pltpu.make_async_copy(k_hbm, kb.at[own, :], s_in.at[0]),
        pltpu.make_async_copy(v_hbm, vb.at[own, :], s_in.at[1]),
        pltpu.make_async_copy(q_hbm, qv, s_in.at[2]),
        pltpu.make_async_copy(g_hbm, gv, s_in.at[3]),
    ]
    own_rows = pl.ds(pl.multiple_of(z * tb, tb), tb)
    for j in range(nj):
        loads.append(pltpu.make_async_copy(h_hbm.at[:, pl.ds(j * dj, dj)], hid.at[j, own_rows, :], s_in.at[4]))
        loads.append(pltpu.make_async_copy(w_hbm.at[:, pl.ds(j * dj, dj)], wv.at[j], s_in.at[5 + j * 4 // nj]))
    for copy in loads:
        copy.start()

    barrier = pltpu.get_barrier_semaphore()
    for c in range(1, nc):
        pl.semaphore_signal(barrier, inc=1, device_id={"col": (z + c) % nc}, device_id_type=MESH)
    for r in range(1, nr):
        pl.semaphore_signal(barrier, inc=1, device_id={"row": (row + r) % nr}, device_id_type=MESH)
    pl.semaphore_signal(barrier, inc=1, device_id={"rollout": core}, device_id_type=MESH)
    pl.semaphore_signal(barrier, inc=1, device_id={"rollout": yside}, device_id_type=MESH)
    for h in range(1, nh + 1):
        @pl.when(dev >= h)
        def _(h=h):
            pl.semaphore_signal(barrier, inc=1, device_id=at(dev - h), device_id_type=MESH)

        @pl.when(dev + h < group)
        def _(h=h):
            pl.semaphore_signal(barrier, inc=1, device_id=at(dev + h), device_id_type=MESH)
    peers = nc - 1 + nr - 1 + 2
    for h in range(1, nh + 1):
        peers = peers + jnp.where(dev >= h, 1, 0) + jnp.where(dev + h < group, 1, 0)
    pl.semaphore_wait(barrier, peers)

    def halo(h, i):
        src, dst = ((k_hbm, kb), (v_hbm, vb))[i]
        return pltpu.make_async_remote_copy(
            src_ref=src, dst_ref=dst.at[pl.ds((nh - h) * td, td), :],
            send_sem=s_halo.at[h - 1, i], recv_sem=r_halo.at[h - 1, i],
            device_id=at(lax.rem(dev + h, group)), device_id_type=MESH,
        )

    for h in range(1, nh + 1):
        @pl.when(dev + h < group)
        def _(h=h):
            halo(h, 0).start()
            halo(h, 1).start()

    def plane_rows(p):
        return pl.ds(pl.multiple_of(p * tb, tb), tb)

    def gather(up, hop, j):
        plane = z - (hop - 1) if up else z + (hop - 1)
        src = h_hbm.at[:, pl.ds(pl.multiple_of(j * dj, dj), dj)] if hop == 1 else hid.at[j, plane_rows(plane), :]
        return pltpu.make_async_remote_copy(
            src_ref=src, dst_ref=hid.at[j, plane_rows(plane), :],
            send_sem=s_g.at[0 if up else 1, hop - 1], recv_sem=r_g.at[0 if up else 1, hop - 1, j],
            device_id={"col": z + 1 if up else z - 1}, device_id_type=MESH,
        )

    def gather_sends(up, hop):
        return (z < nc - 1) & (z >= hop - 1) if up else (z > 0) & (z + hop - 1 < nc)

    def gather_lands(up, hop):
        return z >= hop if up else z + hop < nc

    def gather_start(hop, j):
        for up in (True, False):
            @pl.when(gather_sends(up, hop))
            def _(up=up):
                gather(up, hop, j).start()

    def gather_wait(hop, j, relays):
        for up in (True, False):
            on = gather_sends(up, hop + 1) if hop < nc - 1 else jnp.bool_(False)
            on = on if relays else jnp.logical_not(on)

            @pl.when(gather_lands(up, hop) & on)
            def _(up=up):
                plane = z - hop if up else z + hop
                pltpu.make_async_remote_copy(
                    src_ref=hid.at[j, plane_rows(plane), :], dst_ref=hid.at[j, plane_rows(plane), :],
                    send_sem=s_g.at[0 if up else 1, hop - 1], recv_sem=r_g.at[0 if up else 1, hop - 1, j],
                    device_id={"col": z}, device_id_type=MESH,
                ).wait_recv()

    for j in range(first):
        gather_start(1, j)

    pos = dev * td + lax.broadcasted_iota(jnp.int32, (td, 1), 0)
    bound, parts, start = jnp.int32(0), jnp.zeros((td, 1), jnp.int32), jnp.zeros((td, 1), jnp.int32)
    for i in range(2 * ROLLS):
        bound = bound + lengths_ref[0, i]
        reached = pos >= bound
        parts = parts + reached.astype(jnp.int32)
        if i % 2:
            start = jnp.where(reached, bound, start)
    resp[...] = (parts % 2).astype(jnp.float32)
    shape = (td, (nh + 1) * td)
    col = lax.broadcasted_iota(jnp.int32, shape, 1) + (dev - nh) * td
    line = lax.broadcasted_iota(jnp.int32, shape, 0) + dev * td
    bias[...] = jnp.where((col <= line) & (col >= start), 0.0, -jnp.inf)

    for h in range(1, nh + 1):
        rows = pl.ds((nh - h) * td, td)

        @pl.when(dev < h)
        def _(rows=rows):
            kb[rows, :] = jnp.zeros((td, kw), kb.dtype)
            vb[rows, :] = jnp.zeros((td, kw), vb.dtype)

        @pl.when(dev >= h)
        def _(h=h):
            halo(h, 0).wait_recv()
            halo(h, 1).wait_recv()
    for copy in loads[:4]:
        copy.wait()

    per = HQ // KV

    def send_q1(p):
        return pltpu.make_async_remote_copy(
            src_ref=qv.at[:, pl.ds(pl.multiple_of(p * fp, fp), fp)],
            dst_ref=a1.at[pl.ds(pl.multiple_of(dev * td, td), td), :],
            send_sem=s_q1.at[p], recv_sem=r_q1.at[dev],
            device_id={"col": p}, device_id_type=MESH,
        )

    def nth(i):
        return jnp.where(z < nc // 2, KV - 1 - i, i)

    def block(i, _):
        m = jnp.where(i == KV - 1, z, jnp.where(nth(i) == z, nth(KV - 1), nth(i))) if nc == KV else i
        reads = jnp.full((1, HD), order_ref[m], jnp.int32)
        k = jnp.zeros(((nh + 1) * td, HD), jnp.float32)
        v = jnp.zeros(((nh + 1) * td, HD), jnp.float32)
        for c in range(KV):
            k = jnp.where(reads == c, kb[:, c * HD : (c + 1) * HD].astype(jnp.float32), k)
            v = jnp.where(reads == c, vb[:, c * HD : (c + 1) * HD].astype(jnp.float32), v)
        k, v = k.astype(jnp.bfloat16), v.astype(jnp.bfloat16)
        dk = jnp.zeros(((nh + 1) * td, HD), jnp.float32)
        dv = jnp.zeros(((nh + 1) * td, HD), jnp.float32)
        tall = per
        while tall * (nh + 1) > 2 * per:
            tall //= 2
        mask = jnp.concatenate([bias[...]] * tall, axis=0)
        for low in range(0, per, tall):
            columns = [pl.ds(pl.multiple_of((m * per + hh) * HD, HD), HD) for hh in range(low, low + tall)]
            q = jnp.concatenate([qv[:, cols] for cols in columns], axis=0)
            g = jnp.concatenate(
                [(gv[:, cols].astype(jnp.float32) * resp[...]).astype(jnp.bfloat16) for cols in columns], axis=0
            )
            s = dot_nt(q, k) * scale + mask
            e = jnp.exp(s - jnp.max(s, axis=1, keepdims=True))
            p = e * (1.0 / jnp.sum(e, axis=1, keepdims=True))
            dp = dot_nt(g, v)
            delta = jnp.sum(p * dp, axis=1, keepdims=True)
            ds = (p * (dp - delta) * scale).astype(jnp.bfloat16)
            new = dot32(ds, k).astype(jnp.bfloat16)
            dk = dk + dot_tn(ds, q)
            dv = dv + dot_tn(p.astype(jnp.bfloat16), g)
            for i, cols in enumerate(columns):
                qv[:, cols] = new[i * td : (i + 1) * td]
        dka[:, pl.ds(pl.multiple_of(m * HD, HD), HD)] = dk
        dka[:, pl.ds(pl.multiple_of(kw + m * HD, HD), HD)] = dv
        if nc == KV:
            @pl.when(m != z)
            def _():
                send_q1(m).start()
        return 0

    lax.fori_loop(0, KV, block, 0)
    if nc != KV:
        for c in range(1, nc):
            send_q1((z + c) % nc).start()

    for p in range(nc):
        for b in range(1, nc):
            o = (p + b) % nc
            dq2[p, :, (b - 1) * fb : b * fb] = qv[:, o * fp + p * fb : o * fp + (p + 1) * fb]

    paired = nc == 4

    def send_q2(p):
        rows = pl.ds(pl.multiple_of(dev * td, td), td)
        return pltpu.make_async_remote_copy(
            src_ref=dq2.at[p], dst_ref=a2.at[rows, :], send_sem=s_q2.at[p], recv_sem=r_q2.at[dev],
            device_id={"col": p}, device_id_type=MESH,
        )

    def send_q2_part(p):
        rows = pl.ds(pl.multiple_of(dev * td, td), td)
        kept = pl.ds(pl.multiple_of((1 - p % 2) * fb, fb), 2 * fb)
        return pltpu.make_async_remote_copy(
            src_ref=dq2.at[p, :, kept], dst_ref=a2.at[rows, kept], send_sem=s_q2.at[p], recv_sem=r_q2.at[dev],
            device_id={"col": p}, device_id_type=MESH,
        )

    def each_q2(act):
        for c in range(1, nc):
            p = (z + c) % nc
            if not paired:
                act(send_q2(p))
                continue

            @pl.when(p // 2 == z // 2)
            def _(p=p):
                act(send_q2(p))

            @pl.when(p // 2 != z // 2)
            def _(p=p):
                act(send_q2_part(p))

    def hand_on(d):
        sibling = z ^ 1
        rows = pl.ds(pl.multiple_of(d * td, td), td)
        return pltpu.make_async_remote_copy(
            src_ref=a1.at[rows, pl.ds(pl.multiple_of(sibling * fb, fb), fb)],
            dst_ref=a2.at[rows, pl.ds(pl.multiple_of((sibling % 2) * 2 * fb, fb), fb)],
            send_sem=s_f3.at[d % nc], recv_sem=r_q2.at[d],
            device_id={"col": sibling}, device_id_type=MESH,
        )

    for j in range(first, early):
        gather_start(1, j)
    inner = (z > 0) & (z < nc - 1)

    def send_second():
        each_q2(lambda copy: copy.start())

    def dk_copy(h):
        return pltpu.make_async_remote_copy(
            src_ref=dks.at[h - 1], dst_ref=dkr.at[h - 1], send_sem=s_dk.at[h - 1], recv_sem=r_dk.at[h - 1],
            device_id=at(lax.rem(dev - h + group, group)), device_id_type=MESH,
        )

    for h in range(1, nh + 1):
        dks[h - 1] = dka[(nh - h) * td : (nh - h + 1) * td, :].astype(jnp.bfloat16)

        @pl.when(dev >= h)
        def _(h=h):
            dk_copy(h).start()

    def piece(d):
        return pl.ds(pl.multiple_of(d * td, td), td)

    def over1(d, r):
        return pltpu.make_async_remote_copy(
            src_ref=a1.at[piece(d), :], dst_ref=a1.at[piece(d), :], send_sem=s_f1.at[d % nc, r], recv_sem=r_q1.at[d],
            device_id={"row": (row + r) % nr}, device_id_type=MESH,
        )

    def over2(d, r):
        return pltpu.make_async_remote_copy(
            src_ref=a2.at[piece(d), :], dst_ref=a2.at[piece(d), :],
            send_sem=s_f2.at[d % nc, r], recv_sem=r_q2.at[d],
            device_id={"row": (row + r) % nr}, device_id_type=MESH,
        )

    def spread(over):
        for r in range(1, nr):
            over(dev, r).start()
        for c in (2, -2, 3, -3, 1, -1) if nc == 4 else range(1, nc):
            other = z + c if nc == 4 else (z + c) % nc

            @pl.when((other >= 0) & (other < nc))
            def _(other=other):
                d = row * nc + other
                over(d, 0).wait_recv()
                for r in range(1, nr):
                    over(d, r).start()
                if over is over1 and paired:
                    @pl.when(other // 2 != z // 2)
                    def _():
                        hand_on(d).start()

    def landed(over):
        for r in range(1, nr):
            for c in range(nc):
                over(((row + r) % nr) * nc + c, 0).wait_recv()

    a1[piece(dev), :] = qv[:, pl.ds(pl.multiple_of(z * fp, fp), fp)]
    a2[piece(dev), :] = dq2[z]
    spread(over1)

    more = max(1, MORE * nj // CHUNKS)

    @pl.when(inner)
    def _():
        send_second()
        for j in range(early, more):
            gather_start(1, j)

    landed(over1)

    def second_map():
        landed(over2)
        for r in range(group * td // tb):
            rows = slice(r * tb, (r + 1) * tb)
            a2t[0:fb, rows] = a1[rows, pl.ds(pl.multiple_of(z * fb, fb), fb)].T
            a2t[fb:, rows] = a2[rows, :].T

    def slot(up, t):
        return jnp.where(up == 0, t - 1, t)

    half = tb // 4

    def rs_copy(way, t, j, part):
        at_slot = rs.at[way, slot(way, t), j, pl.ds(part * half, half), :]
        return pltpu.make_async_remote_copy(
            src_ref=at_slot, dst_ref=at_slot, send_sem=s_rs.at[way, slot(way, t)], recv_sem=r_rs.at[way, slot(way, t), j, part],
            device_id={"col": jnp.where(way == 0, z + 1, z - 1)}, device_id_type=MESH,
        )

    def term(t, j):
        return dot32(a1[plane_rows(t), :], wv[j])

    def rs_sends(j, first, last):
        def one(i, _):
            way = (i + z // (nc // 2)) % 2
            t = jnp.where(way == 0, nc - 1 - i // 2, i // 2)
            lands = jnp.where(way == 0, z > 0, z < nc - 1)
            sends = jnp.where(way == 0, t > z, t < z)

            @pl.when(sends)
            def _():
                total = term(t, j)
                for part in range(4):
                    rows = pl.ds(part * half, half)
                    mine = total[part * half : (part + 1) * half]

                    @pl.when(lands)
                    def _(part=part, rows=rows, mine=mine):
                        rs_copy(way, t, j, part).wait_recv()
                        rs[way, slot(way, t), j, rows, :] = (
                            mine + rs[way, slot(way, t), j, rows, :].astype(jnp.float32)
                        ).astype(jnp.bfloat16)

                    @pl.when(jnp.logical_not(lands))
                    def _(rows=rows, mine=mine):
                        rs[way, slot(way, t), j, rows, :] = mine.astype(jnp.bfloat16)

                    rs_copy(way, t, j, part).start()
            return 0

        lax.fori_loop(first, last, one, 0)

    way_z, slot_z = jnp.where(z > 0, 0, 1), jnp.where(z > 0, z - 1, 0)

    def rs_final(j):
        part = term(z, j)

        @pl.when(z > 0)
        def _():
            for i in range(4):
                rs_copy(0, z, j, i).wait_recv()

        @pl.when(z < nc - 1)
        def _():
            for i in range(4):
                rs_copy(1, z, j, i).wait_recv()

        first = part + rs[way_z, slot_z, j].astype(jnp.float32)

        @pl.when((z > 0) & (z < nc - 1))
        def _():
            ig[j] = (first + rs[1, z, j].astype(jnp.float32)).astype(jnp.bfloat16)

        @pl.when((z == 0) | (z == nc - 1))
        def _():
            ig[j] = first.astype(jnp.bfloat16)

    def wterm(o, j):
        b = lax.rem(o - z + nc, nc)
        return dot32(a2t[pl.ds(pl.multiple_of(b * fb, fb), fb), :], hid[j])

    def w1_copy(i, j):
        return pltpu.make_async_remote_copy(
            src_ref=w1s.at[i, j], dst_ref=w1r.at[i, j], send_sem=s_w1.at[i], recv_sem=r_w1.at[i, j],
            device_id={"rollout": core}, device_id_type=MESH,
        )

    def w2_copy(j):
        return pltpu.make_async_remote_copy(
            src_ref=w2s.at[j], dst_ref=w2r.at[j], send_sem=s_w2.at[0], recv_sem=r_w2.at[j],
            device_id={"rollout": yside}, device_id_type=MESH,
        )

    def weight1(j):
        for hop in range(1, nc):
            gather_wait(hop, j, False)

        def one(i, _):
            w1s[i, j] = wterm(core ^ (2 * i), j).astype(jnp.bfloat16)
            w1_copy(i, j).start()
            return 0

        lax.fori_loop(0, 2, one, 0)

    def weight2(j):
        part = wterm(yside, j)
        w1_copy(1, j).wait_recv()
        w2s[j] = (part + w1r[1, j].astype(jnp.float32)).astype(jnp.bfloat16)
        w2_copy(j).start()

    def weight3(j):
        part = wterm(ro, j)
        w1_copy(0, j).wait_recv()
        w2_copy(j).wait_recv()
        wo[j] = part + w1r[0, j].astype(jnp.float32) + w2r[j].astype(jnp.float32)

    def relay(hop, j):
        gather_wait(hop, j, True)
        gather_start(hop + 1, j)

    pltpu.make_async_copy(hid.at[:, own_rows, :], hid.at[:, own_rows, :], s_in.at[4]).wait()
    for i in range(4):
        quarter = wv.at[pl.ds(i * nj // 4, nj // 4)]
        pltpu.make_async_copy(quarter, quarter, s_in.at[5 + i]).wait()
    for j in range(lead1):
        relay(1, j)

    def step(j, _):
        @pl.when(j < nj - lead1)
        def _():
            relay(1, j + lead1)

        begun = j + jnp.where(inner, more, early)

        @pl.when(begun < nj)
        def _():
            gather_start(1, begun)

        for hop in range(2, nc - 1):
            @pl.when((j > 0) & (j < nj - lead2))
            def _(hop=hop):
                relay(hop, j + lead2)

        @pl.when(j < nj)
        def _():
            rs_sends(j, 0, 2)

        for hop in range(2, nc - 1):
            @pl.when(j == 0)
            def _(hop=hop):
                for i in range(lead2 + 1):
                    relay(hop, i)

        @pl.when(j < nj)
        def _():
            rs_sends(j, 2, 2 * (nc - 1))

        @pl.when(j == 0)
        def _():
            @pl.when(jnp.logical_not(inner))
            def _():
                send_second()

            spread(over2)

        @pl.when(j == 1)
        def _():
            second_map()

        @pl.when(inner & (j == 1))
        def _():
            weight1(0)
            weight1(1)
            weight2(0)

        ahead = j + jnp.where(inner, 1, -1)

        @pl.when((ahead >= jnp.where(inner, 2, 1)) & (ahead <= nj))
        def _():
            weight2(ahead - 1)

        @pl.when((j >= 1) & (ahead < nj))
        def _():
            weight1(ahead)

        @pl.when(j >= 3)
        def _():
            rs_final(j - 3)

        behind = j - jnp.where(inner, 2, 3)

        @pl.when((behind >= 0) & (behind < nj))
        def _():
            weight3(behind)
        return 0

    lax.fori_loop(0, nj + 3, step, 0)

    for h in range(1, nh + 1):
        @pl.when(dev + h < group)
        def _(h=h):
            dk_copy(h).wait_recv()
            dka[pl.ds(nh * td, td), :] = dka[pl.ds(nh * td, td), :] + dkr[h - 1].astype(jnp.float32)
    kv_ref[...] = dka[pl.ds(nh * td, td), :]

    for h in range(1, nh + 1):
        @pl.when(dev + h < group)
        def _(h=h):
            halo(h, 0).wait_send()
            halo(h, 1).wait_send()

        @pl.when(dev >= h)
        def _(h=h):
            dk_copy(h).wait_send()
    for c in range(1, nc):
        send_q1((z + c) % nc).wait_send()
        if paired:
            @pl.when((z + c) % nc // 2 != z // 2)
            def _(c=c):
                hand_on(row * nc + (z + c) % nc).wait_send()
    each_q2(lambda copy: copy.wait_send())
    for over in (over1, over2):
        for r in range(1, nr):
            for c in range(nc):
                over(row * nc + c, r).wait_send()

    def sent(ref, sem):
        pltpu.make_async_copy(ref, ref, sem).wait()

    for hop in range(1, nc):
        for up in (True, False):
            @pl.when(gather_sends(up, hop))
            def _(hop=hop, up=up):
                sent(hid.at[:, own_rows, :], s_g.at[0 if up else 1, hop - 1])
    for way in range(2):
        for t in range(way == 0, nc - way):
            @pl.when(t > z if way == 0 else t < z)
            def _(way=way, t=t):
                sent(rs.at[0, 0], s_rs.at[way, slot(way, t)])
    for i in range(2):
        sent(w1s.at[i], s_w1.at[i])
    sent(w2s, s_w2.at[0])


def place_kernel(order_ref, kv, ig, wo, kg_out, vg_out, ig_out, wg_out, placed, s_out):
    kw = kv.shape[1] // 2
    nj, dj = wo.shape[0], wo.shape[2]
    outs = []
    for i, (chunks, out) in enumerate(((wo, wg_out), (ig, ig_out))):
        for j in range(nj):
            outs.append(pltpu.make_async_copy(chunks.at[j], out.at[:, pl.ds(j * dj, dj)], s_out.at[i, j]))
    for copy in outs:
        copy.start()
    for i, out in enumerate((kg_out, vg_out)):
        for c in range(KV):
            total = jnp.zeros((kv.shape[0], HD), jnp.float32)
            for m in range(KV):
                mine = kv[:, i * kw + m * HD : i * kw + (m + 1) * HD]
                total = jnp.where(jnp.full((1, HD), order_ref[m], jnp.int32) == c, mine, total)
            placed[i, :, c * HD : (c + 1) * HD] = total
        copy = pltpu.make_async_copy(placed.at[i], out, s_out.at[2, i])
        copy.start()
        outs.append(copy)
    for copy in outs:
        copy.wait()


def body(queries, keys, values, out_grad, hidden_in, q_weight, lengths, kv_order):
    nr, nc, nro = lax.axis_size("row"), lax.axis_size("col"), lax.axis_size("rollout")
    td, group = queries.shape[0], nr * nc
    length = td * group
    tb, width = hidden_in.shape
    fp = q_weight.shape[0]
    fb = fp // nro
    nj = min(CHUNKS, width // 128)
    dj = width // nj
    nh = -(-(2 * (length // ROLLS) - 1) // td)
    kw = KV * HD
    bf, f32, dma = jnp.bfloat16, jnp.float32, pltpu.SemaphoreType.DMA
    hbm, smem, vmem = (pl.BlockSpec(memory_space=m) for m in (pl.ANY, pltpu.SMEM, pltpu.VMEM))
    call = pl.pallas_call(
        functools.partial(step_kernel, (nc, nr, td, tb, fp, fb, dj, nh, nj)),
        out_shape=(
            pltpu.VMEM((td, 2 * kw), f32),
            pltpu.VMEM((nj, tb, dj), bf),
            pltpu.VMEM((nj, fb, dj), f32),
        ),
        in_specs=[smem, smem] + [hbm] * 6,
        out_specs=(vmem,) * 3,
        scratch_shapes=[
            pltpu.VMEM((td, HQ * HD), bf),
            pltpu.VMEM((td, HQ * HD), bf),
            pltpu.VMEM(((nh + 1) * td, kw), bf),
            pltpu.VMEM(((nh + 1) * td, kw), bf),
            pltpu.VMEM((td, (nh + 1) * td), f32),
            pltpu.VMEM((td, 1), f32),
            pltpu.VMEM((nc, td, (nc - 1) * fb), bf),
            pltpu.VMEM((length, fp), bf),
            pltpu.VMEM((length, (nc - 1) * fb), bf),
            pltpu.VMEM((nc * fb, length), bf),
            pltpu.VMEM((nj, length, dj), bf),
            pltpu.VMEM((nj, fp, dj), bf),
            pltpu.VMEM((2, nc - 1, nj, tb, dj), bf),
            pltpu.VMEM((2, nj, fb, dj), bf),
            pltpu.VMEM((2, nj, fb, dj), bf),
            pltpu.VMEM((nj, fb, dj), bf),
            pltpu.VMEM((nj, fb, dj), bf),
            pltpu.VMEM(((nh + 1) * td, 2 * kw), f32),
            pltpu.VMEM((nh, td, 2 * kw), bf),
            pltpu.VMEM((nh, td, 2 * kw), bf),
            dma((9,)),
            dma((nh, 2)), dma((nh, 2)),
            dma((2, nc - 1)), dma((2, nc - 1, nj)),
            dma((nc,)), dma((group,)), dma((nc, nr)),
            dma((nc,)), dma((group,)), dma((nc, nr)), dma((nc,)),
            dma((2, nc - 1)), dma((2, nc - 1, nj, 4)),
            dma((2,)), dma((2, nj)), dma((1,)), dma((nj,)),
            dma((nh,)), dma((nh,)),
        ],
        compiler_params=pltpu.CompilerParams(
            collective_id=0, has_side_effects=True, vmem_limit_bytes=67043328 - 4 * fb * width - 2 * tb * width - 8 * td * kw - (1 << 17)
        ),
        name="step",
    )
    kv, ig, wg = call(kv_order, lengths, queries, keys, values, out_grad, hidden_in, q_weight)
    place = pl.pallas_call(
        place_kernel,
        out_shape=(
            jax.ShapeDtypeStruct((td, kw), f32),
            jax.ShapeDtypeStruct((td, kw), f32),
            jax.ShapeDtypeStruct((tb, width), bf),
            jax.ShapeDtypeStruct((fb, width), f32),
        ),
        in_specs=[smem, vmem, vmem, vmem],
        out_specs=(hbm,) * 4,
        scratch_shapes=[pltpu.VMEM((2, td, kw), f32), dma((3, nj))],
        compiler_params=pltpu.CompilerParams(vmem_limit_bytes=1 << 22),
        name="place",
    )
    return place(kv_order, *(pltpu.with_memory_space_constraint(x, pltpu.VMEM) for x in (kv, ig, wg)))


def solution(mesh):
    return jax.shard_map(
        body,
        mesh=mesh,
        in_specs=(
            P(("rollout", "row", "col"), None),
            P(("rollout", "row", "col"), None),
            P(("rollout", "row", "col"), None),
            P(("rollout", "row", "col"), None),
            P(("rollout", "col"), "row"),
            P("col", "row"),
            P("rollout", None),
            P(),
        ),
        out_specs=(
            P(("rollout", "row", "col"), None),
            P(("rollout", "row", "col"), None),
            P(("rollout", "col"), "row"),
            P(("rollout", "col"), "row"),
        ),
        check_vma=False,
    )
```
